512 devices in a mesh: seq: 64 (over x, y, z_lo), tp: 8 (over z_hi, core).
Axes of the slice: x: 4, y: 8, z: 8 (z_hi: 4, z_lo: 2; z = z_hi * 2 + z_lo), core: 2. Of those that a mesh axis runs over, the one named last changes fastest.
Arguments:
- queries: bfloat16 [16384, 3072], P(('seq', 'tp')), may hold values from -42 to 42
- keys: bfloat16 [16384, 3072], P(('seq', 'tp')), may hold values from -6 to 6
- values: bfloat16 [16384, 3072], P(('seq', 'tp')), may hold values from -6 to 6
- pool_keys: bfloat16 [64, 128, 3072], P('seq', None, 'tp'), may hold values from -6 to 6
- pool_values: bfloat16 [64, 128, 3072], P('seq', None, 'tp'), may hold values from -6 to 6
- page_table: int32 [64], replicated, may hold values from 0 to 63, each once
- lengths: int32 [128], replicated, may hold values from 1 to 256, 16384 in all
- group_of: int32 [128], replicated, may hold values from 0 to 1
Outputs:
- context: bfloat16 [16384, 3072], P(('seq', 'tp'))
- new_keys: bfloat16 [16384, 3072], P('seq', 'tp')
- new_values: bfloat16 [16384, 3072], P('seq', 'tp')
The draws below stay inside these ranges and needn't reach their ends.
Inputs may be any that keep to these rules, and one draw needn't show every extreme that they name: `page_table`: each of the 64 slots appears once; entries g * 32 to (g + 1) * 32 - 1 are group g's pages; slot s lies on index s of seq. The lengths sum to 16384; each request's suffix tokens follow those of the requests before it.
All inputs are finite; a program needn't handle non-finite values.
Results may differ from the reference program's by a relative error of at most 0.0055.
Values may be sent and summed in bfloat16 or wider, within the bound.
A program may use at most 64 MiB of HBM per device.

```python
import math
import jax
import jax.numpy as jnp
import numpy as np
from jax import lax

H = 32
HD = 96
ROT = 24
PAGE = 128
SUF_MAX = 256
TOK_DEV = 256
C = 3072
TOKENS = 16384
REQS = 128
SLOTS = 64
PAGES_GROUP = 32
PREFIX = 4096


def draw_queries(key, part):
    base_key = jax.random.fold_in(key, 21)
    entries = jnp.clip(2.5 * jax.random.normal(base_key, (TOKENS, C), jnp.float32), -7.5, 7.5)
    return entries.astype(jnp.bfloat16)


def draw_pool_keys(key, part):
    base_key = jax.random.fold_in(key, 31)
    entries = jnp.clip(jax.random.normal(base_key, (SLOTS * PAGE, C), jnp.float32), -6.0, 6.0)
    return entries.reshape(SLOTS, PAGE, C).astype(jnp.bfloat16)


def set_ends(values, key, smallest, largest):
    longest = values.shape.index(max(values.shape))
    spots = []
    for shift in (0, 1):
        where = [jax.random.randint(jax.random.fold_in(key, axis), (), 0, length) for axis, length in enumerate(values.shape)]
        where[longest] = (where[longest] + shift) % values.shape[longest]
        spots.append(tuple(where))
    return values.at[spots[0]].set(smallest).at[spots[1]].set(largest)


def steps_of(rng, dims, pieces, smallest, high):
    level = 1.0
    for dim, parts in pieces:
        steps = jax.random.uniform(jax.random.fold_in(jax.random.fold_in(rng, 6), dim), (parts,), jnp.float32, smallest / len(pieces), high / len(pieces))
        level = level * jnp.repeat(jnp.exp(steps), dims[dim] // parts).reshape((-1,) + (1,) * (len(dims) - 1 - dim))
    return level


def split_up(amount, total, reach, lean):
    weights = [(1 << 20) // math.isqrt(grade ** lean) + 1 for grade in range(2, amount + 1)]
    rest, given = total - reach - (amount - 1), [1] * (amount - 1)
    while rest > 0:
        free = [i for i in range(amount - 1) if given[i] < reach]
        pool, budget = sum([weights[i] for i in free]), rest
        for i in free:
            more = min(reach - given[i], max(1, budget * weights[i] // pool), rest)
            given[i] = given[i] + more
            rest = rest - more
    return np.array([reach] + given)


def uneven(stream_key, number_of, total, limit, slope):
    if number_of == 2:
        one = jax.random.randint(stream_key, (), max(1, total - limit), min(limit, total - 1) + 1)
        return jnp.stack([one, total - one])
    sizes = jnp.asarray(split_up(number_of, total, limit, slope), jnp.int32)
    couples = (number_of - 1) // 2
    source_of, receiver = sizes[1:1 + 2 * couples:2], sizes[2:2 + 2 * couples:2]
    room = jnp.minimum(source_of - 1, limit - receiver)
    moved = jax.random.randint(jax.random.fold_in(stream_key, 1), (couples,), 0, 1 << 20) % (room + 1)
    sizes = sizes.at[1:1 + 2 * couples:2].set(source_of - moved).at[2:2 + 2 * couples:2].set(receiver + moved)
    return sizes[jax.random.permutation(jax.random.fold_in(stream_key, 2), number_of)]


def gaussian(rng, shape, scale, bound, split=(), held_as=jnp.bfloat16):
    gain = steps_of(rng, shape, split, -0.22, 0.18) if split else 1.0
    values = jax.random.normal(rng, shape, jnp.float32) * scale * gain
    return jnp.minimum(jnp.maximum(values, -bound), bound).astype(held_as)


def setup_inputs(seed: int = 0) -> dict:
    key_list = jax.random.split(jax.random.key(seed), 9)
    return {
        "queries": draw_queries(jax.random.fold_in(key_list[8], 71), 0),
        "keys": gaussian(key_list[1], (TOKENS, C), 1.0, 6.0, ((0, 512),)),
        "values": gaussian(key_list[2], (TOKENS, C), 1.0, 6.0, ((0, 512),)),
        "pool_keys": draw_pool_keys(jax.random.fold_in(key_list[8], 71), 0),
        "pool_values": gaussian(key_list[4], (SLOTS, PAGE, C), 1.0, 6.0, ((0, 64), (2, 8))),
        "page_table": jax.random.permutation(key_list[5], SLOTS).astype(jnp.int32),
        "lengths": uneven(key_list[6], REQS, TOKENS, SUF_MAX, 2).astype(jnp.int32),
        "group_of": set_ends(jax.random.randint(key_list[7], (REQS,), 0, 2), jax.random.fold_in(key_list[7], 1), 0, 1).astype(jnp.int32),
    }


def rotate(matrix, position):
    count = matrix.shape[0]
    split_heads = matrix.reshape(count, -1, HD)
    half_rot = ROT // 2
    inverse_freq = 10000.0 ** (-(jnp.arange(half_rot, dtype=jnp.float32) * 2.0 / ROT))
    angles = position.astype(jnp.float32)[:, None] * inverse_freq[None, :]
    cosine = jnp.cos(angles)[:, None, :]
    sine = jnp.sin(angles)[:, None, :]
    first_half = split_heads[..., :half_rot]
    second_half = split_heads[..., half_rot:ROT]
    rest_dims = split_heads[..., ROT:]
    turned = jnp.concatenate([first_half * cosine - second_half * sine, second_half * cosine + first_half * sine, rest_dims], axis=-1)
    return turned.reshape(count, -1)


def reference(queries, keys, values, pool_keys, pool_values, page_table, lengths, group_of):
    request_ends = jnp.cumsum(lengths).astype(jnp.int32)
    request_starts = (request_ends - lengths).astype(jnp.int32)
    token_rows = jnp.arange(TOKENS, dtype=jnp.int32)
    request_of = jnp.sum((token_rows[:, None] >= request_ends[None, :]).astype(jnp.int32), axis=1).astype(jnp.int32)
    offset_of = (token_rows - request_starts[request_of]).astype(jnp.int32)
    token_group = group_of[request_of]
    position = (PREFIX + offset_of).astype(jnp.int32)
    rot_queries = rotate(queries.astype(jnp.float32), position).astype(jnp.bfloat16)
    new_keys = rotate(keys.astype(jnp.float32), position).astype(jnp.bfloat16)
    slot_ids = jnp.arange(SLOTS, dtype=jnp.int32)
    slot_group = jnp.zeros((SLOTS,), jnp.int32).at[page_table].set((slot_ids >= PAGES_GROUP).astype(jnp.int32))
    key_group = jnp.repeat(slot_group, PAGE)
    pool_key_heads = pool_keys.reshape(SLOTS * PAGE, H, HD).astype(jnp.float32)
    pool_value_heads = pool_values.reshape(SLOTS * PAGE, H, HD).astype(jnp.float32)
    padded_keys = jnp.concatenate([jnp.zeros((TOK_DEV, C), jnp.bfloat16), new_keys], axis=0)
    padded_values = jnp.concatenate([jnp.zeros((TOK_DEV, C), jnp.bfloat16), values], axis=0)
    padded_request = jnp.concatenate([jnp.full((TOK_DEV,), -1, jnp.int32), request_of], axis=0)
    score_scale = HD ** -0.5

    def one_block(block_index):
        start = (block_index * TOK_DEV).astype(jnp.int32)
        query_block = lax.dynamic_slice_in_dim(rot_queries, start, TOK_DEV, 0).astype(jnp.float32).reshape(TOK_DEV, H, HD)
        query_request = lax.dynamic_slice_in_dim(request_of, start, TOK_DEV, 0)
        query_group = lax.dynamic_slice_in_dim(token_group, start, TOK_DEV, 0)
        near_keys = lax.dynamic_slice_in_dim(padded_keys, start, 2 * TOK_DEV, 0).astype(jnp.float32).reshape(2 * TOK_DEV, H, HD)
        near_values = lax.dynamic_slice_in_dim(padded_values, start, 2 * TOK_DEV, 0).astype(jnp.float32).reshape(2 * TOK_DEV, H, HD)
        near_request = lax.dynamic_slice_in_dim(padded_request, start, 2 * TOK_DEV, 0)
        key_rows = start - TOK_DEV + jnp.arange(2 * TOK_DEV, dtype=jnp.int32)
        query_rows = start + jnp.arange(TOK_DEV, dtype=jnp.int32)
        near_mask = (near_request[None, :] == query_request[:, None]) & (key_rows[None, :] <= query_rows[:, None])
        pool_mask = key_group[None, :] == query_group[:, None]
        all_keys = jnp.concatenate([pool_key_heads, near_keys], axis=0)
        all_values = jnp.concatenate([pool_value_heads, near_values], axis=0)
        allowed = jnp.concatenate([pool_mask, near_mask], axis=1)
        scores = jnp.einsum('qhd,khd->hqk', query_block, all_keys) * score_scale
        scores = jnp.where(allowed[None], scores, -1e30)
        row_max = jnp.max(scores, axis=-1, keepdims=True)
        weights = jnp.where(allowed[None], jnp.exp(scores - row_max), 0.0)
        total = jnp.sum(weights, axis=-1)
        weights_bf16 = lax.optimization_barrier(weights.astype(jnp.bfloat16)).astype(jnp.float32)
        output = jnp.einsum('hqk,khd->hqd', weights_bf16, all_values) / total[..., None]
        return output.transpose(1, 0, 2).reshape(TOK_DEV, C).astype(jnp.bfloat16)

    blocks = lax.map(one_block, jnp.arange(TOKENS // TOK_DEV, dtype=jnp.int32))
    context = blocks.reshape(TOKENS, C)
    return context, new_keys, values
```

```python
import jax
import jax.numpy as jnp
from jax import lax
from jax.experimental import pallas as pl
from jax.experimental.pallas import tpu as pltpu
from jax.sharding import PartitionSpec as P

MESH = pl.DeviceIdType.MESH
HD = 96
ROT = 24
HALF = ROT // 2
HEADS = 4
CH = HEADS * HD
TOK = 256
PART = 32
NT = 8
NX, NY, NZ = 4, 8, 2
COL = NY * NZ
PAGE = 128
KEYS = COL * PAGE
SEQ = NX * NY * NZ
NEG = -1e30
EXP_SCALE = HD**-0.5 * 1.4426950408889634
VMEM = pltpu.VMEM


def where_am_i():
    s = lax.axis_index("seq")
    t = lax.axis_index("tp")
    x = s // COL
    y = (s // NZ) % NY
    z = s % NZ
    return s, t, x, y, z


def greet(peers):
    barrier = pltpu.get_barrier_semaphore()
    for peer in peers:
        pl.semaphore_signal(barrier, inc=1, device_id=peer, device_id_type=MESH)
    pl.semaphore_wait(barrier, len(peers))


def remote(src, dst, send, recv, peer):
    return pltpu.make_async_remote_copy(
        src_ref=src, dst_ref=dst, send_sem=send, recv_sem=recv, device_id=peer, device_id_type=MESH
    )


def spread_kernel(
    q_ref, k_ref, v_ref, pk_ref, pv_ref,
    qa_ref, k2_ref, v2_ref, gk_ref, gv_ref,
    a_send, a_recv, z_send, z_recv, r_send, r_recv, x_send, x_recv, s_send, s_recv, loc,
):
    s, t, x, y, z = where_am_i()
    col = s % COL
    partner = (s + 1 - 2 * z, t)
    up = (x * COL + ((y + 1) % NY) * NZ + z, t)
    down = (x * COL + ((y + NY - 1) % NY) * NZ + z, t)
    after = ((s + 1) % SEQ, t)
    before = ((s + SEQ - 1) % SEQ, t)
    tps = [(s, (t + j) % NT) for j in range(1, NT)]
    xs = [(((x + j) % NX) * COL + col, t) for j in range(1, NX)]
    greet([partner, up, down, after, before] + tps + xs)

    pending = []

    def go(copy):
        copy.start()
        pending.append(copy)
        return copy

    zk = go(remote(pk_ref.at[0], gk_ref.at[y, z], z_send.at[0], z_recv.at[0], partner))
    zv = go(remote(pv_ref.at[0], gv_ref.at[y, z], z_send.at[1], z_recv.at[1], partner))

    def rows(ref, kind):
        return ref.at[x if kind == 0 else 1, pl.ds(pl.multiple_of(t * PART, PART), PART), :]

    def lanes(ref, index):
        return ref.at[:, pl.ds(pl.multiple_of(index * CH, 128), CH)]

    kinds = [(q_ref, qa_ref), (k_ref, k2_ref), (v_ref, v2_ref)]
    swaps = []
    for kind, (src, dst) in enumerate(kinds):
        swaps.append(
            [
                go(remote(lanes(src, tps[j][1]), rows(dst, kind), a_send.at[kind, j], a_recv.at[kind, j], tps[j]))
                for j in range(NT - 1)
            ]
        )
    own = [
        pltpu.make_async_copy(pk_ref.at[0], gk_ref.at[y, z], loc.at[0]),
        pltpu.make_async_copy(pv_ref.at[0], gv_ref.at[y, z], loc.at[1]),
    ] + [
        pltpu.make_async_copy(lanes(src, t), rows(dst, kind), loc.at[2 + kind])
        for kind, (src, dst) in enumerate(kinds)
    ]
    for copy in own:
        copy.start()
    for copy in own:
        copy.wait()
    zk.wait_recv()
    zv.wait_recv()

    flows = [(gk_ref, 0, 4), (gv_ref, 0, 3), (gk_ref, 1, 3), (gv_ref, 1, 4)]
    last = [None] * len(flows)

    def hop(step):
        for index, (ref, way, hops) in enumerate(flows):
            if step > 0 and last[index] is not None:
                last[index].wait_recv()
                last[index] = None
            if step < hops:
                at = (y + NY - step) % NY if way == 0 else (y + step) % NY
                last[index] = go(
                    remote(
                        ref.at[at], ref.at[at], r_send.at[index, step], r_recv.at[index, step], up if way == 0 else down
                    )
                )

    hop(0)
    for copy in swaps[0]:
        copy.wait_recv()
    across = [
        go(remote(qa_ref.at[x], qa_ref.at[x], x_send.at[j], x_recv.at[j], xs[j])) for j in range(NX - 1)
    ]
    hop(1)
    for copy in swaps[1] + swaps[2]:
        copy.wait_recv()
    shifts = [
        go(remote(ref.at[1], ref.at[0], s_send.at[i], s_recv.at[i], after)) for i, ref in enumerate((k2_ref, v2_ref))
    ]
    hop(2)
    hop(3)
    hop(4)
    for copy in across + shifts:
        copy.wait_recv()
    for copy in pending:
        copy.wait_send()


def spread(q, k, v, pk, pv):
    bf = jnp.bfloat16
    dma = pltpu.SemaphoreType.DMA
    return pl.pallas_call(
        spread_kernel,
        out_shape=(
            jax.ShapeDtypeStruct((NX, TOK, CH), bf),
            jax.ShapeDtypeStruct((2, TOK, CH), bf),
            jax.ShapeDtypeStruct((2, TOK, CH), bf),
            jax.ShapeDtypeStruct((NY, NZ, PAGE, CH), bf),
            jax.ShapeDtypeStruct((NY, NZ, PAGE, CH), bf),
        ),
        in_specs=[pl.BlockSpec(memory_space=VMEM)] * 5,
        out_specs=[pl.BlockSpec(memory_space=VMEM)] * 5,
        scratch_shapes=[
            dma((3, NT - 1)), dma((3, NT - 1)),
            dma((2,)), dma((2,)),
            dma((4, 4)), dma((4, 4)),
            dma((NX - 1,)), dma((NX - 1,)),
            dma((2,)), dma((2,)),
            dma((5,)),
        ],
        compiler_params=pltpu.CompilerParams(collective_id=0, has_side_effects=True),
        name="spread",
    )(q, k, v, pk, pv)


def turn(matrix, cosine, sine):
    parts = []
    for h in range(HEADS):
        lead = matrix[h * HD : h * HD + ROT]
        other = jnp.concatenate([lead[HALF:], lead[:HALF]], axis=0)
        parts += [lead * cosine + other * sine, matrix[h * HD + ROT : (h + 1) * HD]]
    return jnp.concatenate(parts, axis=0)


def widen(columns, h):
    start = h * HD - (h // 2) * 128
    pieces = []
    if start:
        pieces.append(jnp.zeros((start, TOK), jnp.bfloat16))
    pieces.append(columns[h * HD : (h + 1) * HD])
    if start + HD < 256:
        pieces.append(jnp.zeros((256 - start - HD, TOK), jnp.bfloat16))
    return jnp.concatenate(pieces, axis=0)


def attend_kernel(
    qa_ref, k2_ref, v2_ref, gk_ref, gv_ref, cos_ref, sin_ref, bias_ref, offset_ref,
    o_ref, stat_ref, osuf_ref, ssuf_ref, newk_ref,
    vt_ref, vs_ref, ks_ref,
):
    me = lax.axis_index("seq") // COL
    for b in range(2):
        turned = turn(k2_ref[b].astype(jnp.float32).T, cos_ref[b], sin_ref[b])
        turned = turned.T.astype(jnp.bfloat16)
        ks_ref[b * TOK : (b + 1) * TOK, :] = turned
        vs_ref[:, b * TOK : (b + 1) * TOK] = v2_ref[b].astype(jnp.float32).T.astype(jnp.bfloat16)
    newk_ref[...] = ks_ref[TOK:, :]
    for b in range(KEYS // 256):
        vt_ref[:, b * 256 : (b + 1) * 256] = (
            gv_ref[b * 256 : (b + 1) * 256, :].astype(jnp.float32).T.astype(jnp.bfloat16)
        )

    def queries(b):
        return turn(qa_ref[b].astype(jnp.float32).T, cos_ref[2 + b], sin_ref[2 + b]).astype(jnp.bfloat16)

    def finish(scores, values):
        top = jnp.max(scores, axis=0, keepdims=True)
        weights = jnp.exp2((scores - top) * EXP_SCALE)
        total = jnp.sum(weights, axis=0, keepdims=True)
        summed = jnp.dot(values, weights.astype(jnp.bfloat16), preferred_element_type=jnp.float32)
        return top, total, summed / total

    def one_block(b, carry):
        columns = queries(b)
        bias = bias_ref[b]
        for h in range(HEADS):
            lane = (h // 2) * 128
            scores = jnp.dot(gk_ref[:, lane : lane + 256], widen(columns, h), preferred_element_type=jnp.float32)
            scores = (scores.reshape(COL, PAGE, TOK) + bias[:, None, :]).reshape(KEYS, TOK)
            top, total, out = finish(scores, vt_ref[h * HD : (h + 1) * HD, :])
            o_ref[b, h * HD : (h + 1) * HD, :] = out.astype(jnp.bfloat16)
            stat_ref[b, h : h + 1, :] = top
            stat_ref[b, HEADS + h : HEADS + h + 1, :] = total
        return carry

    lax.fori_loop(0, NX, one_block, 0)

    columns = queries(me)
    token = lax.broadcasted_iota(jnp.int32, (2 * TOK, TOK), 1) + TOK
    key = lax.broadcasted_iota(jnp.int32, (2 * TOK, TOK), 0)
    allowed = (key <= token) & (key >= token - offset_ref[...])
    for h in range(HEADS):
        lane = (h // 2) * 128
        scores = jnp.dot(ks_ref[:, lane : lane + 256], widen(columns, h), preferred_element_type=jnp.float32)
        scores = jnp.where(allowed, scores, NEG)
        top, total, out = finish(scores, vs_ref[h * HD : (h + 1) * HD, :])
        osuf_ref[h * HD : (h + 1) * HD, :] = out
        ssuf_ref[h : h + 1, :] = top
        ssuf_ref[HEADS + h : HEADS + h + 1, :] = total


def attend(qa, k2, v2, gk, gv, cosine, sine, bias, offset):
    f32, bf = jnp.float32, jnp.bfloat16
    return pl.pallas_call(
        attend_kernel,
        out_shape=(
            jax.ShapeDtypeStruct((NX, CH, TOK), bf),
            jax.ShapeDtypeStruct((NX, 2 * HEADS, TOK), f32),
            jax.ShapeDtypeStruct((CH, TOK), f32),
            jax.ShapeDtypeStruct((2 * HEADS, TOK), f32),
            jax.ShapeDtypeStruct((TOK, CH), bf),
        ),
        in_specs=[pl.BlockSpec(memory_space=VMEM)] * 9,
        out_specs=[pl.BlockSpec(memory_space=VMEM)] * 5,
        scratch_shapes=[
            VMEM((CH, KEYS), bf),
            VMEM((CH, 2 * TOK), bf),
            VMEM((2 * TOK, CH), bf),
        ],
        name="attend",
    )(qa, k2, v2, gk, gv, cosine, sine, bias, offset)


def merge_kernel(
    o_ref, stat_ref, osuf_ref, ssuf_ref, out_ref,
    ro_ref, rs_ref, c_ref, o_send, o_recv, t_send, t_recv, a_send, a_recv, loc,
):
    s, t, x, y, z = where_am_i()
    col = s % COL
    tps = [(s, (t + j) % NT) for j in range(1, NT)]
    there = [(x + j) % NX for j in range(1, NX)]
    xs = [(w * COL + col, t) for w in there]
    greet(tps + xs)
    copies = []
    for j in range(NX - 1):
        copies.append(remote(stat_ref.at[there[j]], rs_ref.at[j], t_send.at[j], t_recv.at[j], xs[j]))
        copies.append(remote(o_ref.at[there[j]], ro_ref.at[j], o_send.at[j], o_recv.at[j], xs[j]))
    for copy in copies:
        copy.start()
    for copy in copies:
        copy.wait_recv()
    stats = [ssuf_ref[...], stat_ref[x]] + [rs_ref[j] for j in range(NX - 1)]
    top = stats[0][:HEADS]
    for st in stats[1:]:
        top = jnp.maximum(top, st[:HEADS])
    scales = [jnp.exp2((st[:HEADS] - top) * EXP_SCALE) * st[HEADS:] for st in stats]
    total = scales[0] + scales[1] + scales[2] + scales[3] + scales[4]
    scales = [sc / total for sc in scales]
    heads = []
    for h in range(HEADS):
        part = slice(h * HD, (h + 1) * HD)
        acc = osuf_ref[part, :] * scales[0][h : h + 1]
        acc += o_ref[x, part, :].astype(jnp.float32) * scales[1][h : h + 1]
        for j in range(NX - 1):
            acc += ro_ref[j, part, :].astype(jnp.float32) * scales[2 + j][h : h + 1]
        heads.append(acc)
    c_ref[...] = jnp.concatenate(heads, axis=0).T.astype(jnp.bfloat16)

    def rows(index):
        return c_ref.at[pl.ds(pl.multiple_of(index * PART, PART), PART), :]

    place = out_ref.at[:, pl.ds(pl.multiple_of(t * CH, 128), CH)]
    back = [remote(rows(tps[j][1]), place, a_send.at[j], a_recv.at[j], tps[j]) for j in range(NT - 1)]
    for copy in back:
        copy.start()
    mine = pltpu.make_async_copy(rows(t), place, loc.at[0])
    mine.start()
    mine.wait()
    for copy in back:
        copy.wait_recv()
    for copy in copies + back:
        copy.wait_send()


def merge(o, stat, osuf, ssuf):
    dma = pltpu.SemaphoreType.DMA
    return pl.pallas_call(
        merge_kernel,
        out_shape=jax.ShapeDtypeStruct((PART, NT * CH), jnp.bfloat16),
        in_specs=[pl.BlockSpec(memory_space=VMEM)] * 4,
        out_specs=pl.BlockSpec(memory_space=VMEM),
        scratch_shapes=[
            VMEM((NX - 1, CH, TOK), jnp.bfloat16),
            VMEM((NX - 1, 2 * HEADS, TOK), jnp.float32),
            VMEM((TOK, CH), jnp.bfloat16),
            dma((NX - 1,)), dma((NX - 1,)),
            dma((NX - 1,)), dma((NX - 1,)),
            dma((NT - 1,)), dma((NT - 1,)),
            dma((1,)),
        ],
        compiler_params=pltpu.CompilerParams(collective_id=1, has_side_effects=True),
        name="merge",
    )(o, stat, osuf, ssuf)


def tables(page_table, lengths, group_of):
    s = lax.axis_index("seq")
    x, col = s // COL, s % COL
    blocks = jnp.concatenate([jnp.stack([s - 1, s]), jnp.arange(NX, dtype=jnp.int32) * COL + col])
    rows = (blocks[:, None] * TOK + jnp.arange(TOK, dtype=jnp.int32)[None, :]).astype(jnp.int32)
    starts = (jnp.cumsum(lengths) - lengths).astype(jnp.int32)
    begun = starts[:, None, None] <= rows[None]
    first = jnp.max(jnp.where(begun, starts[:, None, None], 0), axis=0)
    ids = jnp.arange(lengths.shape[0], dtype=jnp.int32)
    request = jnp.sum(begun.astype(jnp.int32), axis=0) - 1
    group = jnp.sum(jnp.where(request[None] == ids[:, None, None], group_of[:, None, None], 0), axis=0)
    offset = rows - first
    position = (COL * NX * PAGE // 2 + offset).astype(jnp.float32)
    inverse_freq = 10000.0 ** (-(jnp.arange(HALF, dtype=jnp.float32) * 2.0 / ROT))
    angles = position[:, None, :] * inverse_freq[None, :, None]
    cosine, sine = jnp.cos(angles), jnp.sin(angles)
    slots = x * COL + jnp.arange(COL, dtype=jnp.int32)
    late = page_table[page_table.shape[0] // 2 :]
    slot_group = jnp.any(slots[:, None] == late[None, :], axis=1).astype(jnp.int32)
    bias = jnp.where(group[2:, None, :] == slot_group[None, :, None], 0.0, NEG).astype(jnp.float32)
    return (
        jnp.concatenate([cosine, cosine], axis=1),
        jnp.concatenate([-sine, sine], axis=1),
        bias,
        offset[1][None, :],
    )


def local(queries, keys, values, pool_keys, pool_values, page_table, lengths, group_of):
    cosine, sine, bias, offset = tables(page_table, lengths, group_of)
    qa, k2, v2, gk, gv = spread(queries, keys, values, pool_keys, pool_values)
    o, stat, osuf, ssuf, new_keys = attend(
        qa, k2, v2, gk.reshape(KEYS, CH), gv.reshape(KEYS, CH), cosine, sine, bias, offset
    )
    context = merge(o, stat, osuf, ssuf)
    return context, new_keys, v2[1]


def solution(mesh):
    return jax.shard_map(
        local,
        mesh=mesh,
        in_specs=(
            P(("seq", "tp"), None),
            P(("seq", "tp"), None),
            P(("seq", "tp"), None),
            P("seq", None, "tp"),
            P("seq", None, "tp"),
            P(),
            P(),
            P(),
        ),
        out_specs=(P(("seq", "tp"), None), P("seq", "tp"), P("seq", "tp")),
        check_vma=False,
    )
```

```python
import jax
import jax.numpy as jnp
from jax import lax
from jax.experimental import pallas as pl
from jax.experimental.pallas import tpu as pltpu
from jax.sharding import PartitionSpec as P

MESH = pl.DeviceIdType.MESH
HD = 96
ROT = 24
HALF = ROT // 2
HEADS = 4
CH = HEADS * HD
TOK = 256
PART = 32
NT = 8
NX, NY, NZ = 4, 8, 2
COL = NY * NZ
PAGE = 128
KEYS = COL * PAGE
SEQ = NX * NY * NZ
NEG = -1e30
EXP_SCALE = HD**-0.5 * 1.4426950408889634
VMEM = pltpu.VMEM


def where_am_i():
    s = lax.axis_index("seq")
    t = lax.axis_index("tp")
    x = s // COL
    y = (s // NZ) % NY
    z = s % NZ
    return s, t, x, y, z


def greet(peers):
    barrier = pltpu.get_barrier_semaphore()
    for peer in peers:
        pl.semaphore_signal(barrier, inc=1, device_id=peer, device_id_type=MESH)
    pl.semaphore_wait(barrier, len(peers))


def remote(src, dst, send, recv, peer):
    return pltpu.make_async_remote_copy(
        src_ref=src, dst_ref=dst, send_sem=send, recv_sem=recv, device_id=peer, device_id_type=MESH
    )


def spread_kernel(
    q_ref, k_ref, v_ref, pk_ref, pv_ref,
    qa_ref, k2_ref, v2_ref, gk_ref, gv_ref,
    a_send, a_recv, z_send, z_recv, r_send, r_recv, y_send, y_recv, x_send, x_recv, s_send, s_recv, loc,
):
    s, t, x, y, z = where_am_i()
    col = s % COL
    partner = (s + 1 - 2 * z, t)
    up = (x * COL + ((y + 1) % NY) * NZ + z, t)
    down = (x * COL + ((y + NY - 1) % NY) * NZ + z, t)
    east = (((x + 1) % NX) * COL + col, t)
    west = (((x + NX - 1) % NX) * COL + col, t)
    after = ((s + 1) % SEQ, t)
    before = ((s + SEQ - 1) % SEQ, t)
    tps = [(s, (t + j) % NT) for j in range(1, NT)]
    greet([partner, up, down, east, west, after, before] + tps)

    pending = []

    def go(copy):
        copy.start()
        pending.append(copy)
        return copy

    low, high = pl.ds(0, PAGE // 2), pl.ds(PAGE // 2, PAGE // 2)
    zk = go(remote(pk_ref.at[0], gk_ref.at[y, z], z_send.at[0], z_recv.at[0], partner))
    zv = go(remote(pv_ref.at[0, low], gv_ref.at[y, z, low], z_send.at[1], z_recv.at[1], partner))

    def rows(ref, kind):
        return ref.at[x if kind == 0 else 1, pl.ds(pl.multiple_of(t * PART, PART), PART), :]

    def lanes(ref, index):
        return ref.at[:, pl.ds(pl.multiple_of(index * CH, 128), CH)]

    kinds = [(q_ref, qa_ref), (k_ref, k2_ref), (v_ref, v2_ref)]
    own = [
        pltpu.make_async_copy(pk_ref.at[0], gk_ref.at[y, z], loc.at[0]),
        pltpu.make_async_copy(pv_ref.at[0], gv_ref.at[y, z], loc.at[1]),
    ] + [
        pltpu.make_async_copy(lanes(src, t), rows(dst, kind), loc.at[2 + kind])
        for kind, (src, dst) in enumerate(kinds)
    ]
    for copy in own:
        copy.start()
    swaps = []
    for kind, (src, dst) in enumerate(kinds):
        swaps.append(
            [
                go(remote(lanes(src, tps[j][1]), rows(dst, kind), a_send.at[kind, j], a_recv.at[kind, j], tps[j]))
                for j in range(NT - 1)
            ]
        )
    for copy in own:
        copy.wait()

    flows = [(gk_ref, 0, 4), (gv_ref, 0, 3), (gk_ref, 1, 3), (gv_ref, 1, 4)]
    last = [None] * len(flows)
    single = [None, None]
    handed = []

    def index_of(way, step):
        return (y + NY - step) % NY if way == 0 else (y + step) % NY

    def hop_single(step):
        for way, hops in ((0, 4), (1, 3)):
            block = gv_ref.at[index_of(way, step), z, high]
            if single[way] is not None:
                single[way].wait_recv()
                single[way] = None
            if step < hops:
                single[way] = go(
                    remote(block, block, y_send.at[way, step], y_recv.at[way, step], up if way == 0 else down)
                )
            if step <= hops and (way == 0 or step > 0):
                handed.append(go(remote(block, block, y_send.at[2 + way, step], y_recv.at[2 + way, step], partner)))

    def hop(step):
        hop_single(step)
        if step == 0:
            zk.wait_recv()
            zv.wait_recv()
        for index, (ref, way, hops) in enumerate(flows):
            if last[index] is not None:
                last[index].wait_recv()
                last[index] = None
            if step < hops:
                at = index_of(way, step)
                block = ref.at[at] if ref is gk_ref else ref.at[at, :, low]
                last[index] = go(
                    remote(block, block, r_send.at[index, step], r_recv.at[index, step], up if way == 0 else down)
                )

    hop(0)
    for copy in swaps[0]:
        copy.wait_recv()
    across = [
        go(remote(qa_ref.at[x], qa_ref.at[x], x_send.at[i], x_recv.at[i], to)) for i, to in enumerate((east, west))
    ]
    hop(1)
    relays = []
    for i, to in enumerate((east, west)):
        across[i].wait_recv()
        half = qa_ref.at[(x + NX - 1) % NX if i == 0 else (x + 1) % NX, pl.ds(i * (TOK // 2), TOK // 2), :]
        relays.append(go(remote(half, half, x_send.at[2 + i], x_recv.at[2 + i], to)))
    for copy in swaps[1] + swaps[2]:
        copy.wait_recv()
    shifts = [
        go(remote(ref.at[1], ref.at[0], s_send.at[i], s_recv.at[i], after)) for i, ref in enumerate((k2_ref, v2_ref))
    ]
    hop(2)
    hop(3)
    hop(4)
    for copy in relays + shifts + handed:
        copy.wait_recv()
    for copy in pending:
        copy.wait_send()


def spread(q, k, v, pk, pv):
    bf = jnp.bfloat16
    dma = pltpu.SemaphoreType.DMA
    return pl.pallas_call(
        spread_kernel,
        out_shape=(
            jax.ShapeDtypeStruct((NX, TOK, CH), bf),
            jax.ShapeDtypeStruct((2, TOK, CH), bf),
            jax.ShapeDtypeStruct((2, TOK, CH), bf),
            jax.ShapeDtypeStruct((NY, NZ, PAGE, CH), bf),
            jax.ShapeDtypeStruct((NY, NZ, PAGE, CH), bf),
        ),
        in_specs=[pl.BlockSpec(memory_space=VMEM)] * 5,
        out_specs=[pl.BlockSpec(memory_space=VMEM)] * 5,
        scratch_shapes=[
            dma((3, NT - 1)), dma((3, NT - 1)),
            dma((2,)), dma((2,)),
            dma((4, 4)), dma((4, 4)),
            dma((4, 5)), dma((4, 5)),
            dma((4,)), dma((4,)),
            dma((2,)), dma((2,)),
            dma((5,)),
        ],
        compiler_params=pltpu.CompilerParams(collective_id=0, has_side_effects=True),
        name="spread",
    )(q, k, v, pk, pv)


def turn(matrix, cosine, sine):
    parts = []
    for h in range(HEADS):
        lead = matrix[h * HD : h * HD + ROT]
        other = jnp.concatenate([lead[HALF:], lead[:HALF]], axis=0)
        parts += [lead * cosine + other * sine, matrix[h * HD + ROT : (h + 1) * HD]]
    return jnp.concatenate(parts, axis=0)


def widen(columns, h):
    start = h * HD - (h // 2) * 128
    pieces = []
    if start:
        pieces.append(jnp.zeros((start, TOK), jnp.bfloat16))
    pieces.append(columns[h * HD : (h + 1) * HD])
    if start + HD < 256:
        pieces.append(jnp.zeros((256 - start - HD, TOK), jnp.bfloat16))
    return jnp.concatenate(pieces, axis=0)


def attend_kernel(
    qa_ref, k2_ref, v2_ref, gk_ref, gv_ref, cos_ref, sin_ref, bias_ref, offset_ref,
    out_ref, newk_ref,
    vt_ref, vs_ref, ks_ref, o_ref, stat_ref, ro_ref, rs_ref, c_ref,
    o_send, o_recv, t_send, t_recv, a_send, a_recv, loc,
):
    s, t, x, y, z = where_am_i()
    col = s % COL
    tps = [(s, (t + j) % NT) for j in range(1, NT)]
    peers = tps + [(((x + j) % NX) * COL + col, t) for j in range(1, NX)]
    barrier = pltpu.get_barrier_semaphore()
    for peer in peers:
        pl.semaphore_signal(barrier, inc=1, device_id=peer, device_id_type=MESH)

    for b in range(2):
        turned = turn(k2_ref[b].astype(jnp.float32).T, cos_ref[b], sin_ref[b])
        turned = turned.T.astype(jnp.bfloat16)
        ks_ref[b * TOK : (b + 1) * TOK, :] = turned
        vs_ref[:, b * TOK : (b + 1) * TOK] = v2_ref[b].astype(jnp.float32).T.astype(jnp.bfloat16)
    newk_ref[...] = ks_ref[TOK:, :]
    for b in range(KEYS // 256):
        vt_ref[:, b * 256 : (b + 1) * 256] = (
            gv_ref[b * 256 : (b + 1) * 256, :].astype(jnp.float32).T.astype(jnp.bfloat16)
        )
    pl.semaphore_wait(barrier, len(peers))

    def queries(b):
        return turn(qa_ref[b].astype(jnp.float32).T, cos_ref[2 + b], sin_ref[2 + b]).astype(jnp.bfloat16)

    def finish(scores, values):
        top = jnp.max(scores, axis=0, keepdims=True)
        weights = jnp.exp2((scores - top) * EXP_SCALE)
        total = jnp.sum(weights, axis=0, keepdims=True)
        summed = jnp.dot(values, weights.astype(jnp.bfloat16), preferred_element_type=jnp.float32)
        return top, total, summed / total

    def hand_over(j):
        b = (x + NX - 1 - j) % NX
        to = (b * COL + col, t)
        return [
            remote(stat_ref.at[b], rs_ref.at[j], t_send.at[j], t_recv.at[j], to),
            remote(o_ref.at[b], ro_ref.at[j], o_send.at[j], o_recv.at[j], to),
        ]

    def one_block(j, carry):
        b = (x + NX - 1 - j) % NX
        columns = queries(b)
        bias = bias_ref[b]
        for h in range(HEADS):
            lane = (h // 2) * 128
            scores = jnp.dot(gk_ref[:, lane : lane + 256], widen(columns, h), preferred_element_type=jnp.float32)
            scores = (scores.reshape(COL, PAGE, TOK) + bias[:, None, :]).reshape(KEYS, TOK)
            top, total, out = finish(scores, vt_ref[h * HD : (h + 1) * HD, :])
            o_ref[b, h * HD : (h + 1) * HD, :] = out.astype(jnp.bfloat16)
            stat_ref[b, h : h + 1, :] = top
            stat_ref[b, HEADS + h : HEADS + h + 1, :] = total
            if h == 0:

                @pl.when(j > 0)
                def _():
                    for copy in hand_over(j - 1):
                        copy.start()

        return carry

    lax.fori_loop(0, NX, one_block, 0)

    columns = queries(x)
    token = lax.broadcasted_iota(jnp.int32, (2 * TOK, TOK), 1) + TOK
    key = lax.broadcasted_iota(jnp.int32, (2 * TOK, TOK), 0)
    allowed = (key <= token) & (key >= token - offset_ref[...])
    suffix = []
    for h in range(HEADS):
        lane = (h // 2) * 128
        scores = jnp.dot(ks_ref[:, lane : lane + 256], widen(columns, h), preferred_element_type=jnp.float32)
        scores = jnp.where(allowed, scores, NEG)
        suffix.append(finish(scores, vs_ref[h * HD : (h + 1) * HD, :]))

    copies = [copy for j in range(NX - 1) for copy in hand_over(j)]
    for copy in copies:
        copy.wait_recv()
    heads = []
    for h in range(HEADS):
        part = slice(h * HD, (h + 1) * HD)
        one, two = slice(h, h + 1), slice(HEADS + h, HEADS + h + 1)
        tops = [suffix[h][0], stat_ref[x, one, :]] + [rs_ref[j, one, :] for j in range(NX - 1)]
        totals = [suffix[h][1], stat_ref[x, two, :]] + [rs_ref[j, two, :] for j in range(NX - 1)]
        outs = [suffix[h][2], o_ref[x, part, :]] + [ro_ref[j, part, :] for j in range(NX - 1)]
        top = tops[0]
        for other in tops[1:]:
            top = jnp.maximum(top, other)
        scales = [jnp.exp2((a - top) * EXP_SCALE) * b for a, b in zip(tops, totals)]
        total = scales[0] + scales[1] + scales[2] + scales[3] + scales[4]
        acc = outs[0] * (scales[0] / total)
        for out, scale in zip(outs[1:], scales[1:]):
            acc += out.astype(jnp.float32) * (scale / total)
        heads.append(acc)
    c_ref[...] = jnp.concatenate(heads, axis=0).T.astype(jnp.bfloat16)

    def rows(index):
        return c_ref.at[pl.ds(pl.multiple_of(index * PART, PART), PART), :]

    place = out_ref.at[:, pl.ds(pl.multiple_of(t * CH, 128), CH)]
    back = [remote(rows(tps[j][1]), place, a_send.at[j], a_recv.at[j], tps[j]) for j in range(NT - 1)]
    for copy in back:
        copy.start()
    mine = pltpu.make_async_copy(rows(t), place, loc.at[0])
    mine.start()
    mine.wait()
    for copy in back:
        copy.wait_recv()
    for copy in copies + back:
        copy.wait_send()


def attend(qa, k2, v2, gk, gv, cosine, sine, bias, offset):
    f32, bf = jnp.float32, jnp.bfloat16
    dma = pltpu.SemaphoreType.DMA
    return pl.pallas_call(
        attend_kernel,
        out_shape=(
            jax.ShapeDtypeStruct((PART, NT * CH), bf),
            jax.ShapeDtypeStruct((TOK, CH), bf),
        ),
        in_specs=[pl.BlockSpec(memory_space=VMEM)] * 9,
        out_specs=[pl.BlockSpec(memory_space=VMEM)] * 2,
        scratch_shapes=[
            VMEM((CH, KEYS), bf),
            VMEM((CH, 2 * TOK), bf),
            VMEM((2 * TOK, CH), bf),
            VMEM((NX, CH, TOK), bf),
            VMEM((NX, 2 * HEADS, TOK), f32),
            VMEM((NX - 1, CH, TOK), bf),
            VMEM((NX - 1, 2 * HEADS, TOK), f32),
            VMEM((TOK, CH), bf),
            dma((NX - 1,)), dma((NX - 1,)),
            dma((NX - 1,)), dma((NX - 1,)),
            dma((NT - 1,)), dma((NT - 1,)),
            dma((1,)),
        ],
        compiler_params=pltpu.CompilerParams(collective_id=1, has_side_effects=True),
        name="attend",
    )(qa, k2, v2, gk, gv, cosine, sine, bias, offset)


def tables(page_table, lengths, group_of):
    s = lax.axis_index("seq")
    x, col = s // COL, s % COL
    blocks = jnp.concatenate([jnp.stack([s - 1, s]), jnp.arange(NX, dtype=jnp.int32) * COL + col])
    rows = (blocks[:, None] * TOK + jnp.arange(TOK, dtype=jnp.int32)[None, :]).astype(jnp.int32)
    starts = (jnp.cumsum(lengths) - lengths).astype(jnp.int32)
    begun = starts[:, None, None] <= rows[None]
    first = jnp.max(jnp.where(begun, starts[:, None, None], 0), axis=0)
    ids = jnp.arange(lengths.shape[0], dtype=jnp.int32)
    request = jnp.sum(begun.astype(jnp.int32), axis=0) - 1
    group = jnp.sum(jnp.where(request[None] == ids[:, None, None], group_of[:, None, None], 0), axis=0)
    offset = rows - first
    position = (COL * NX * PAGE // 2 + offset).astype(jnp.float32)
    inverse_freq = 10000.0 ** (-(jnp.arange(HALF, dtype=jnp.float32) * 2.0 / ROT))
    angles = position[:, None, :] * inverse_freq[None, :, None]
    cosine, sine = jnp.cos(angles), jnp.sin(angles)
    slots = x * COL + jnp.arange(COL, dtype=jnp.int32)
    late = page_table[page_table.shape[0] // 2 :]
    slot_group = jnp.any(slots[:, None] == late[None, :], axis=1).astype(jnp.int32)
    bias = jnp.where(group[2:, None, :] == slot_group[None, :, None], 0.0, NEG).astype(jnp.float32)
    return (
        jnp.concatenate([cosine, cosine], axis=1),
        jnp.concatenate([-sine, sine], axis=1),
        bias,
        offset[1][None, :],
    )


def local(queries, keys, values, pool_keys, pool_values, page_table, lengths, group_of):
    cosine, sine, bias, offset = tables(page_table, lengths, group_of)
    qa, k2, v2, gk, gv = spread(queries, keys, values, pool_keys, pool_values)
    context, new_keys = attend(
        qa, k2, v2, gk.reshape(KEYS, CH), gv.reshape(KEYS, CH), cosine, sine, bias, offset
    )
    return context, new_keys, v2[1]


def solution(mesh):
    return jax.shard_map(
        local,
        mesh=mesh,
        in_specs=(
            P(("seq", "tp"), None),
            P(("seq", "tp"), None),
            P(("seq", "tp"), None),
            P("seq", None, "tp"),
            P("seq", None, "tp"),
            P(),
            P(),
            P(),
        ),
        out_specs=(P(("seq", "tp"), None), P("seq", "tp"), P("seq", "tp")),
        check_vma=False,
    )
```

```python
import jax
import jax.numpy as jnp
from jax import lax
from jax.experimental import pallas as pl
from jax.experimental.pallas import tpu as pltpu
from jax.sharding import PartitionSpec as P

MESH = pl.DeviceIdType.MESH
HD = 96
ROT = 24
HALF = ROT // 2
HEADS = 4
CH = HEADS * HD
TOK = 256
PART = 32
NT = 8
NX, NY, NZ = 4, 8, 2
COL = NY * NZ
PAGE = 128
KEYS = COL * PAGE
SEQ = NX * NY * NZ
NEG = -1e30
EXP_SCALE = HD**-0.5 * 1.4426950408889634
VMEM = pltpu.VMEM


def where_am_i():
    s = lax.axis_index("seq")
    t = lax.axis_index("tp")
    x = s // COL
    y = (s // NZ) % NY
    z = s % NZ
    return s, t, x, y, z


def greet(peers):
    barrier = pltpu.get_barrier_semaphore()
    for peer in peers:
        pl.semaphore_signal(barrier, inc=1, device_id=peer, device_id_type=MESH)
    pl.semaphore_wait(barrier, len(peers))


def remote(src, dst, send, recv, peer):
    return pltpu.make_async_remote_copy(
        src_ref=src, dst_ref=dst, send_sem=send, recv_sem=recv, device_id=peer, device_id_type=MESH
    )


def turn(matrix, cosine, sine):
    parts = []
    for h in range(HEADS):
        lead = matrix[h * HD : h * HD + ROT]
        other = jnp.concatenate([lead[HALF:], lead[:HALF]], axis=0)
        parts += [lead * cosine + other * sine, matrix[h * HD + ROT : (h + 1) * HD]]
    return jnp.concatenate(parts, axis=0)


def widen(columns, h):
    start = h * HD - (h // 2) * 128
    pieces = []
    if start:
        pieces.append(jnp.zeros((start, TOK), jnp.bfloat16))
    pieces.append(columns[h * HD : (h + 1) * HD])
    if start + HD < 256:
        pieces.append(jnp.zeros((256 - start - HD, TOK), jnp.bfloat16))
    return jnp.concatenate(pieces, axis=0)


def attend_kernel(
    q_ref, k_ref, v_ref, pk_ref, pv_ref, cos_ref, sin_ref, bias_ref, offset_ref,
    out_ref, newk_ref, newv_ref,
    qa_ref, k2_ref, v2_ref, gk_ref, gv_ref,
    qt_ref, vt_ref, vs_ref, ks_ref, acc_ref, run_ref, o_ref, stat_ref, ro_ref, rs_ref, c_ref,
    a_send, a_recv, z_send, z_recv, r_send, r_recv, y_send, y_recv, x_send, x_recv, s_send, s_recv,
    o_send, o_recv, t_send, t_recv, b_send, b_recv, loc,
):
    s, t, x, y, z = where_am_i()
    col = s % COL
    partner = (s + 1 - 2 * z, t)
    up = (x * COL + ((y + 1) % NY) * NZ + z, t)
    down = (x * COL + ((y + NY - 1) % NY) * NZ + z, t)
    east = (((x + 1) % NX) * COL + col, t)
    west = (((x + NX - 1) % NX) * COL + col, t)
    across_x = (((x + 2) % NX) * COL + col, t)
    after = ((s + 1) % SEQ, t)
    before = ((s + SEQ - 1) % SEQ, t)
    tps = [(s, (t + j) % NT) for j in range(1, NT)]
    greet([partner, up, down, east, west, across_x, after, before] + tps)

    pending = []

    def go(copy):
        copy.start()
        pending.append(copy)
        return copy

    low, high = pl.ds(0, PAGE // 2), pl.ds(PAGE // 2, PAGE // 2)
    zk = go(remote(pk_ref.at[0], gk_ref.at[y, z], z_send.at[0], z_recv.at[0], partner))
    zv = go(remote(pv_ref.at[0, low], gv_ref.at[y, z, low], z_send.at[1], z_recv.at[1], partner))

    def rows(ref, kind):
        return ref.at[x if kind == 0 else 1, pl.ds(pl.multiple_of(t * PART, PART), PART), :]

    def lanes(ref, index):
        return ref.at[:, pl.ds(pl.multiple_of(index * CH, 128), CH)]

    kinds = [(q_ref, qa_ref), (k_ref, k2_ref), (v_ref, v2_ref)]
    own = [
        pltpu.make_async_copy(pk_ref.at[0], gk_ref.at[y, z], loc.at[0]),
        pltpu.make_async_copy(pv_ref.at[0], gv_ref.at[y, z], loc.at[1]),
    ] + [
        pltpu.make_async_copy(lanes(src, t), rows(dst, kind), loc.at[2 + kind])
        for kind, (src, dst) in enumerate(kinds)
    ]
    for copy in own:
        copy.start()
    swaps = []
    for kind, (src, dst) in enumerate(kinds):
        swaps.append(
            [
                go(remote(lanes(src, tps[j][1]), rows(dst, kind), a_send.at[kind, j], a_recv.at[kind, j], tps[j]))
                for j in range(NT - 1)
            ]
        )
    for copy in own:
        copy.wait()

    flows = [(gk_ref, 0, 4), (gv_ref, 0, 3), (gk_ref, 1, 3), (gv_ref, 1, 4)]
    last = [None] * len(flows)
    single = [None, None]
    handed = {}

    def index_of(way, step):
        return (y + NY - step) % NY if way == 0 else (y + step) % NY

    def hop_single(step):
        for way, hops in ((0, 4), (1, 3)):
            block = gv_ref.at[index_of(way, step), z, high]
            if single[way] is not None:
                single[way].wait_recv()
                single[way] = None
            if step < hops:
                single[way] = go(
                    remote(block, block, y_send.at[way, step], y_recv.at[way, step], up if way == 0 else down)
                )
            if step <= hops and (way == 0 or step > 0):
                handed.setdefault(step, []).append(
                    go(remote(block, block, y_send.at[2 + way, step], y_recv.at[2 + way, step], partner))
                )

    def hop(step):
        hop_single(step)
        if step == 0:
            zk.wait_recv()
            zv.wait_recv()
        for index, (ref, way, hops) in enumerate(flows):
            if last[index] is not None:
                last[index].wait_recv()
                last[index] = None
            if step < hops:
                at = index_of(way, step)
                block = ref.at[at] if ref is gk_ref else ref.at[at, :, low]
                last[index] = go(
                    remote(block, block, r_send.at[index, step], r_recv.at[index, step], up if way == 0 else down)
                )

    def prepare(b):
        turned = turn(qa_ref[b].astype(jnp.float32).T, cos_ref[2 + b], sin_ref[2 + b])
        qt_ref[b] = turned.astype(jnp.bfloat16)

    def receive_values(step, places):
        for copy in handed.pop(step, []):
            copy.wait_recv()
        for at in places:
            vt_ref[at] = gv_ref[at].reshape(NZ * PAGE, CH).astype(jnp.float32).T.astype(jnp.bfloat16)

    def score(b, h, at):
        lane = (h // 2) * 128
        keys = gk_ref[at, :, :, lane : lane + 256].reshape(NZ * PAGE, 256)
        scores = jnp.dot(keys, widen(qt_ref[b], h), preferred_element_type=jnp.float32)
        return (scores.reshape(NZ, PAGE, TOK) + bias_ref[b, at][:, None, :]).reshape(NZ * PAGE, TOK)

    def weigh(scores, top, values):
        total, summed = None, None
        for block, value in zip(scores, values):
            weights = jnp.exp2((block - top) * EXP_SCALE)
            part = jnp.sum(weights, axis=0, keepdims=True)
            out = jnp.dot(value, weights.astype(jnp.bfloat16), preferred_element_type=jnp.float32)
            total = part if total is None else total + part
            summed = out if summed is None else summed + out
        return total, summed

    def peak(scores):
        top = jnp.max(scores[0], axis=0, keepdims=True)
        for block in scores[1:]:
            top = jnp.maximum(top, jnp.max(block, axis=0, keepdims=True))
        return top

    def update(b, h, places, first):
        part = slice(h * HD, (h + 1) * HD)
        scores = [score(b, h, at) for at in places]
        top = peak(scores)
        if not first:
            old = run_ref[b, h : h + 1, :]
            top = jnp.maximum(old, top)
        total, summed = weigh(scores, top, [vt_ref[at, part, :] for at in places])
        if not first:
            factor = jnp.exp2((old - top) * EXP_SCALE)
            total += run_ref[b, HEADS + h : HEADS + h + 1, :] * factor
            summed += acc_ref[b, part, :] * factor
        return top, total, summed

    def absorb(places, first=False):
        def one(b, carry):
            for h in range(HEADS):
                top, total, summed = update(b, h, places, first)
                run_ref[b, h : h + 1, :] = top
                run_ref[b, HEADS + h : HEADS + h + 1, :] = total
                acc_ref[b, h * HD : (h + 1) * HD, :] = summed
            return carry

        lax.fori_loop(0, NX, one, 0)

    def ahead(n):
        return (y + n) % NY

    hop(0)
    for copy in swaps[0]:
        copy.wait_recv()
    across = [
        go(remote(qa_ref.at[x], qa_ref.at[x], x_send.at[i], x_recv.at[i], to)) for i, to in enumerate((east, west))
    ]
    prepare(x)
    hop(1)
    relays = []
    for i, to in enumerate((east, west)):
        across[i].wait_recv()
        half = qa_ref.at[(x + NX - 1) % NX if i == 0 else (x + 1) % NX, pl.ds(i * (TOK // 2), TOK // 2), :]
        relays.append(go(remote(half, half, x_send.at[2 + i], x_recv.at[2 + i], to)))
    for copy in swaps[1] + swaps[2]:
        copy.wait_recv()
    shifts = [
        go(remote(ref.at[1], ref.at[0], s_send.at[i], s_recv.at[i], after)) for i, ref in enumerate((k2_ref, v2_ref))
    ]
    newv_ref[...] = v2_ref[1]
    prepare((x + 1) % NX)
    prepare((x + 3) % NX)
    receive_values(0, [y])
    receive_values(1, [ahead(1), ahead(7)])
    for copy in relays:
        copy.wait_recv()
    prepare((x + 2) % NX)
    absorb([y], True)
    hop(2)
    absorb([ahead(1), ahead(7)])
    receive_values(2, [ahead(2), ahead(6)])
    absorb([ahead(2)])
    hop(3)
    absorb([ahead(6)])
    receive_values(3, [ahead(3), ahead(5)])
    absorb([ahead(3), ahead(5)])
    hop(4)
    receive_values(4, [ahead(4)])

    def hand_over(j):
        b = (x + NX - 1 - j) % NX
        to = (b * COL + col, t)
        return [
            remote(stat_ref.at[b], rs_ref.at[j], t_send.at[j], t_recv.at[j], to),
            remote(o_ref.at[b], ro_ref.at[j], o_send.at[j], o_recv.at[j], to),
        ]

    def close(j, carry):
        b = (x + NX - 1 - j) % NX
        for h in range(HEADS):
            top, total, summed = update(b, h, [ahead(4)], False)
            o_ref[b, h * HD : (h + 1) * HD, :] = (summed / total).astype(jnp.bfloat16)
            stat_ref[b, h : h + 1, :] = top
            stat_ref[b, HEADS + h : HEADS + h + 1, :] = total
            if h == 0:

                @pl.when(j > 0)
                def _():
                    for copy in hand_over(j - 1):
                        copy.start()

        return carry

    lax.fori_loop(0, NX, close, 0)

    for copy in shifts:
        copy.wait_recv()
    for b in range(2):
        turned = turn(k2_ref[b].astype(jnp.float32).T, cos_ref[b], sin_ref[b])
        ks_ref[b * TOK : (b + 1) * TOK, :] = turned.T.astype(jnp.bfloat16)
        vs_ref[:, b * TOK : (b + 1) * TOK] = v2_ref[b].astype(jnp.float32).T.astype(jnp.bfloat16)
    newk_ref[...] = ks_ref[TOK:, :]
    columns = qt_ref[x]
    token = lax.broadcasted_iota(jnp.int32, (2 * TOK, TOK), 1) + TOK
    key = lax.broadcasted_iota(jnp.int32, (2 * TOK, TOK), 0)
    allowed = (key <= token) & (key >= token - offset_ref[...])
    suffix = []
    for h in range(HEADS):
        lane = (h // 2) * 128
        scores = jnp.dot(ks_ref[:, lane : lane + 256], widen(columns, h), preferred_element_type=jnp.float32)
        scores = [jnp.where(allowed, scores, NEG)]
        top = peak(scores)
        total, summed = weigh(scores, top, [vs_ref[h * HD : (h + 1) * HD, :]])
        suffix.append((top, total, summed / total))

    copies = [copy for j in range(NX - 1) for copy in hand_over(j)]
    for copy in copies:
        copy.wait_recv()
    heads = []
    for h in range(HEADS):
        part = slice(h * HD, (h + 1) * HD)
        one, two = slice(h, h + 1), slice(HEADS + h, HEADS + h + 1)
        tops = [suffix[h][0], stat_ref[x, one, :]] + [rs_ref[j, one, :] for j in range(NX - 1)]
        totals = [suffix[h][1], stat_ref[x, two, :]] + [rs_ref[j, two, :] for j in range(NX - 1)]
        outs = [suffix[h][2], o_ref[x, part, :]] + [ro_ref[j, part, :] for j in range(NX - 1)]
        top = tops[0]
        for other in tops[1:]:
            top = jnp.maximum(top, other)
        scales = [jnp.exp2((a - top) * EXP_SCALE) * b for a, b in zip(tops, totals)]
        total = scales[0] + scales[1] + scales[2] + scales[3] + scales[4]
        acc = outs[0] * (scales[0] / total)
        for out, scale in zip(outs[1:], scales[1:]):
            acc += out.astype(jnp.float32) * (scale / total)
        heads.append(acc)
    c_ref[...] = jnp.concatenate(heads, axis=0).T.astype(jnp.bfloat16)

    def out_rows(index):
        return c_ref.at[pl.ds(pl.multiple_of(index * PART, PART), PART), :]

    place = out_ref.at[:, pl.ds(pl.multiple_of(t * CH, 128), CH)]
    back = [remote(out_rows(tps[j][1]), place, b_send.at[j], b_recv.at[j], tps[j]) for j in range(NT - 1)]
    for copy in back:
        copy.start()
    mine = pltpu.make_async_copy(out_rows(t), place, loc.at[5])
    mine.start()
    mine.wait()
    for copy in back:
        copy.wait_recv()
    for copy in pending + copies + back:
        copy.wait_send()


def attend(q, k, v, pk, pv, cosine, sine, bias, offset):
    f32, bf = jnp.float32, jnp.bfloat16
    dma = pltpu.SemaphoreType.DMA
    return pl.pallas_call(
        attend_kernel,
        out_shape=(
            jax.ShapeDtypeStruct((PART, NT * CH), bf),
            jax.ShapeDtypeStruct((TOK, CH), bf),
            jax.ShapeDtypeStruct((TOK, CH), bf),
        ),
        in_specs=[pl.BlockSpec(memory_space=VMEM)] * 9,
        out_specs=[pl.BlockSpec(memory_space=VMEM)] * 3,
        scratch_shapes=[
            VMEM((NX, TOK, CH), bf),
            VMEM((2, TOK, CH), bf),
            VMEM((2, TOK, CH), bf),
            VMEM((NY, NZ, PAGE, CH), bf),
            VMEM((NY, NZ, PAGE, CH), bf),
            VMEM((NX, CH, TOK), bf),
            VMEM((NY, CH, NZ * PAGE), bf),
            VMEM((CH, 2 * TOK), bf),
            VMEM((2 * TOK, CH), bf),
            VMEM((NX, CH, TOK), f32),
            VMEM((NX, 2 * HEADS, TOK), f32),
            VMEM((NX, CH, TOK), bf),
            VMEM((NX, 2 * HEADS, TOK), f32),
            VMEM((NX - 1, CH, TOK), bf),
            VMEM((NX - 1, 2 * HEADS, TOK), f32),
            VMEM((TOK, CH), bf),
            dma((3, NT - 1)), dma((3, NT - 1)),
            dma((2,)), dma((2,)),
            dma((4, 4)), dma((4, 4)),
            dma((4, 5)), dma((4, 5)),
            dma((4,)), dma((4,)),
            dma((2,)), dma((2,)),
            dma((NX - 1,)), dma((NX - 1,)),
            dma((NX - 1,)), dma((NX - 1,)),
            dma((NT - 1,)), dma((NT - 1,)),
            dma((6,)),
        ],
        compiler_params=pltpu.CompilerParams(collective_id=0, has_side_effects=True),
        name="attend",
    )(q, k, v, pk, pv, cosine, sine, bias, offset)


def tables(page_table, lengths, group_of):
    s = lax.axis_index("seq")
    x, col = s // COL, s % COL
    blocks = jnp.concatenate([jnp.stack([s - 1, s]), jnp.arange(NX, dtype=jnp.int32) * COL + col])
    rows = (blocks[:, None] * TOK + jnp.arange(TOK, dtype=jnp.int32)[None, :]).astype(jnp.int32)
    starts = (jnp.cumsum(lengths) - lengths).astype(jnp.int32)
    begun = starts[:, None, None] <= rows[None]
    first = jnp.max(jnp.where(begun, starts[:, None, None], 0), axis=0)
    ids = jnp.arange(lengths.shape[0], dtype=jnp.int32)
    request = jnp.sum(begun.astype(jnp.int32), axis=0) - 1
    group = jnp.sum(jnp.where(request[None] == ids[:, None, None], group_of[:, None, None], 0), axis=0)
    offset = rows - first
    position = (COL * NX * PAGE // 2 + offset).astype(jnp.float32)
    inverse_freq = 10000.0 ** (-(jnp.arange(HALF, dtype=jnp.float32) * 2.0 / ROT))
    angles = position[:, None, :] * inverse_freq[None, :, None]
    cosine, sine = jnp.cos(angles), jnp.sin(angles)
    slots = x * COL + jnp.arange(COL, dtype=jnp.int32)
    late = page_table[page_table.shape[0] // 2 :]
    slot_group = jnp.any(slots[:, None] == late[None, :], axis=1).astype(jnp.int32)
    bias = jnp.where(group[2:, None, :] == slot_group[None, :, None], 0.0, NEG).astype(jnp.float32)
    return (
        jnp.concatenate([cosine, cosine], axis=1),
        jnp.concatenate([-sine, sine], axis=1),
        bias.reshape(NX, NY, NZ, TOK),
        offset[1][None, :],
    )


def local(queries, keys, values, pool_keys, pool_values, page_table, lengths, group_of):
    cosine, sine, bias, offset = tables(page_table, lengths, group_of)
    return attend(queries, keys, values, pool_keys, pool_values, cosine, sine, bias, offset)


def solution(mesh):
    return jax.shard_map(
        local,
        mesh=mesh,
        in_specs=(
            P(("seq", "tp"), None),
            P(("seq", "tp"), None),
            P(("seq", "tp"), None),
            P("seq", None, "tp"),
            P("seq", None, "tp"),
            P(),
            P(),
            P(),
        ),
        out_specs=(P(("seq", "tp"), None), P("seq", "tp"), P("seq", "tp")),
        check_vma=False,
    )
```

```python
import jax
import jax.numpy as jnp
import numpy as np
from jax import lax
from jax.experimental import pallas as pl
from jax.experimental.pallas import tpu as pltpu
from jax.sharding import PartitionSpec as P

MESH = pl.DeviceIdType.MESH
HD = 96
ROT = 24
HALF = ROT // 2
HEADS = 4
CH = HEADS * HD
TOK = 256
PART = 32
NT = 8
NX, NY, NZ = 4, 8, 2
COL = NY * NZ
PAGE = 128
KEYS = COL * PAGE
SEQ = NX * NY * NZ
NEG = -1e30
EXP_SCALE = HD**-0.5 * 1.4426950408889634
VMEM = pltpu.VMEM


def where_am_i():
    s = lax.axis_index("seq")
    t = lax.axis_index("tp")
    x = s // COL
    y = (s // NZ) % NY
    z = s % NZ
    return s, t, x, y, z


def greet(peers):
    barrier = pltpu.get_barrier_semaphore()
    for peer in peers:
        pl.semaphore_signal(barrier, inc=1, device_id=peer, device_id_type=MESH)
    pl.semaphore_wait(barrier, len(peers))


def remote(src, dst, send, recv, peer):
    return pltpu.make_async_remote_copy(
        src_ref=src, dst_ref=dst, send_sem=send, recv_sem=recv, device_id=peer, device_id_type=MESH
    )


def turn(matrix, cosine, sine):
    parts = []
    for h in range(HEADS):
        lead = matrix[h * HD : h * HD + ROT]
        other = jnp.concatenate([lead[HALF:], lead[:HALF]], axis=0)
        parts += [lead * cosine + other * sine, matrix[h * HD + ROT : (h + 1) * HD]]
    return jnp.concatenate(parts, axis=0)


def widen(columns, h):
    start = h * HD - (h // 2) * 128
    pieces = []
    if start:
        pieces.append(jnp.zeros((start, TOK), jnp.bfloat16))
    pieces.append(columns[h * HD : (h + 1) * HD])
    if start + HD < 256:
        pieces.append(jnp.zeros((256 - start - HD, TOK), jnp.bfloat16))
    return jnp.concatenate(pieces, axis=0)


def tables(page_ref, length_ref, group_ref, freq_ref, cos_ref, sin_ref, bias_ref, offset_ref):
    s, t, x, y, z = where_am_i()
    f32 = jnp.float32
    count = length_ref.shape[1]
    slots = page_ref.shape[1]
    lane = lax.broadcasted_iota(jnp.int32, (count, count), 1)
    line = lax.broadcasted_iota(jnp.int32, (count, count), 0)
    lengths = jnp.broadcast_to(length_ref[...].astype(f32), (count, count))
    groups = jnp.broadcast_to(group_ref[...].astype(f32), (count, count))
    starts = jnp.sum(jnp.where(lane < line, lengths, 0.0), axis=1, keepdims=True)
    ends = jnp.sum(jnp.where(lane <= line, lengths, 0.0), axis=1, keepdims=True)
    group_of = jnp.sum(jnp.where(lane == line, groups, 0.0), axis=1, keepdims=True)
    slot = lax.broadcasted_iota(jnp.int32, (COL, slots), 0) + x * COL
    place = lax.broadcasted_iota(jnp.int32, (COL, slots), 1)
    page = jnp.broadcast_to(page_ref[...], (COL, slots))
    late = jnp.sum(jnp.where((page == slot) & (place >= slots // 2), 1.0, 0.0), axis=1, keepdims=True)
    sign = jnp.where(lax.broadcasted_iota(jnp.int32, (ROT, TOK), 0) < HALF, -1.0, 1.0)
    for i in range(2 + NX):
        block = s - 1 + i if i < 2 else (i - 2) * COL + s % COL
        rows = (block * TOK + lax.broadcasted_iota(jnp.int32, (1, TOK), 1)).astype(f32)
        begun = starts <= rows
        first = jnp.max(jnp.where(begun, starts, 0.0), axis=0, keepdims=True)
        group = jnp.sum(jnp.where(begun & (rows < ends), group_of, 0.0), axis=0, keepdims=True)
        offset = rows - first
        angles = (COL * NX * PAGE // 2 + offset) * freq_ref[...]
        cos_ref[i] = jnp.cos(angles)
        sin_ref[i] = jnp.sin(angles) * sign
        if i == 1:
            offset_ref[...] = offset.astype(jnp.int32)
        if i >= 2:
            bias = jnp.where(group == late, 0.0, NEG)
            for at in range(NY):
                bias_ref[i - 2, at] = bias[at * NZ : (at + 1) * NZ]


def attend_kernel(
    q_ref, k_ref, v_ref, pk_ref, pv_ref, page_ref, length_ref, group_ref, freq_ref,
    out_ref, newk_ref, newv_ref,
    cos_ref, sin_ref, bias_ref, offset_ref,
    qa_ref, k2_ref, v2_ref, gk_ref, gv_ref,
    qt_ref, vt_ref, vs_ref, ks_ref, acc_ref, run_ref, o_ref, stat_ref, ro_ref, rs_ref, c_ref,
    a_send, a_recv, z_send, z_recv, r_send, r_recv, y_send, y_recv, x_send, x_recv, s_send, s_recv,
    o_send, o_recv, t_send, t_recv, b_send, b_recv, loc,
):
    s, t, x, y, z = where_am_i()
    col = s % COL
    partner = (s + 1 - 2 * z, t)
    up = (x * COL + ((y + 1) % NY) * NZ + z, t)
    down = (x * COL + ((y + NY - 1) % NY) * NZ + z, t)
    east = (((x + 1) % NX) * COL + col, t)
    west = (((x + NX - 1) % NX) * COL + col, t)
    across_x = (((x + 2) % NX) * COL + col, t)
    after = ((s + 1) % SEQ, t)
    before = ((s + SEQ - 1) % SEQ, t)
    tps = [(s, (t + j) % NT) for j in range(1, NT)]
    greet([partner, up, down, east, west, across_x, after, before] + tps)

    pending = []

    def go(copy):
        copy.start()
        pending.append(copy)
        return copy

    low, high = pl.ds(0, PAGE // 2), pl.ds(PAGE // 2, PAGE // 2)
    zk = go(remote(pk_ref.at[0], gk_ref.at[y, z], z_send.at[0], z_recv.at[0], partner))
    zv = go(remote(pv_ref.at[0, low], gv_ref.at[y, z, low], z_send.at[1], z_recv.at[1], partner))

    def rows(ref, kind):
        return ref.at[x if kind == 0 else 1, pl.ds(pl.multiple_of(t * PART, PART), PART), :]

    def lanes(ref, index):
        return ref.at[:, pl.ds(pl.multiple_of(index * CH, 128), CH)]

    kinds = [(q_ref, qa_ref), (k_ref, k2_ref), (v_ref, v2_ref)]
    own = [
        pltpu.make_async_copy(pk_ref.at[0], gk_ref.at[y, z], loc.at[0]),
        pltpu.make_async_copy(pv_ref.at[0], gv_ref.at[y, z], loc.at[1]),
    ] + [
        pltpu.make_async_copy(lanes(src, t), rows(dst, kind), loc.at[2 + kind])
        for kind, (src, dst) in enumerate(kinds)
    ]
    for copy in own:
        copy.start()
    swaps = []
    for kind, (src, dst) in enumerate(kinds):
        swaps.append(
            [
                go(remote(lanes(src, tps[j][1]), rows(dst, kind), a_send.at[kind, j], a_recv.at[kind, j], tps[j]))
                for j in range(NT - 1)
            ]
        )
    for copy in own:
        copy.wait()

    flows = [(gk_ref, 0, 4), (gv_ref, 0, 3), (gk_ref, 1, 3), (gv_ref, 1, 4)]
    last = [None] * len(flows)
    single = [None, None]
    handed = {}

    def index_of(way, step):
        return (y + NY - step) % NY if way == 0 else (y + step) % NY

    def hop_single(step):
        for way, hops in ((0, 4), (1, 3)):
            block = gv_ref.at[index_of(way, step), z, high]
            if single[way] is not None:
                single[way].wait_recv()
                single[way] = None
            if step < hops:
                single[way] = go(
                    remote(block, block, y_send.at[way, step], y_recv.at[way, step], up if way == 0 else down)
                )
            if step <= hops and (way == 0 or step > 0):
                handed.setdefault(step, []).append(
                    go(remote(block, block, y_send.at[2 + way, step], y_recv.at[2 + way, step], partner))
                )

    def hop(step):
        if step > 0:
            hop_single(step)
        else:
            zk.wait_recv()
            zv.wait_recv()
        for index, (ref, way, hops) in enumerate(flows):
            if last[index] is not None:
                last[index].wait_recv()
                last[index] = None
            if step == 1:
                early[index].wait_recv()
            if step < hops:
                at = index_of(way, step)
                which = 1 - z if step == 0 else slice(None)
                block = ref.at[at, which] if ref is gk_ref else ref.at[at, which, low]
                last[index] = go(
                    remote(block, block, r_send.at[index, step], r_recv.at[index, step], up if way == 0 else down)
                )

    def prepare(b):
        turned = turn(qa_ref[b].astype(jnp.float32).T, cos_ref[2 + b], sin_ref[2 + b])
        qt_ref[b] = turned.astype(jnp.bfloat16)

    def receive_values(step, places):
        for copy in handed.pop(step, []):
            copy.wait_recv()
        for at in places:
            vt_ref[at] = gv_ref[at].reshape(NZ * PAGE, CH).astype(jnp.float32).T.astype(jnp.bfloat16)

    def score(b, h, at):
        lane = (h // 2) * 128
        keys = gk_ref[at, :, :, lane : lane + 256].reshape(NZ * PAGE, 256)
        scores = jnp.dot(keys, widen(qt_ref[b], h), preferred_element_type=jnp.float32)
        return (scores.reshape(NZ, PAGE, TOK) + bias_ref[b, at][:, None, :]).reshape(NZ * PAGE, TOK)

    def weigh(scores, top, values):
        total, summed = None, None
        for block, value in zip(scores, values):
            weights = jnp.exp2((block - top) * EXP_SCALE)
            part = jnp.sum(weights, axis=0, keepdims=True)
            out = jnp.dot(value, weights.astype(jnp.bfloat16), preferred_element_type=jnp.float32)
            total = part if total is None else total + part
            summed = out if summed is None else summed + out
        return total, summed

    def peak(scores):
        top = jnp.max(scores[0], axis=0, keepdims=True)
        for block in scores[1:]:
            top = jnp.maximum(top, jnp.max(block, axis=0, keepdims=True))
        return top

    def update(b, h, places, first):
        part = slice(h * HD, (h + 1) * HD)
        scores = [score(b, h, at) for at in places]
        top = peak(scores)
        if not first:
            old = run_ref[b, h : h + 1, :]
            top = jnp.maximum(old, top)
        total, summed = weigh(scores, top, [vt_ref[at, part, :] for at in places])
        if not first:
            factor = jnp.exp2((old - top) * EXP_SCALE)
            total += run_ref[b, HEADS + h : HEADS + h + 1, :] * factor
            summed += acc_ref[b, part, :] * factor
        return top, total, summed

    def absorb(places, first=False):
        def one(b, carry):
            for h in range(HEADS):
                top, total, summed = update(b, h, places, first)
                run_ref[b, h : h + 1, :] = top
                run_ref[b, HEADS + h : HEADS + h + 1, :] = total
                acc_ref[b, h * HD : (h + 1) * HD, :] = summed
            return carry

        lax.fori_loop(0, NX, one, 0)

    def ahead(n):
        return (y + n) % NY

    early = []
    for index, (ref, way, hops) in enumerate(flows):
        block = ref.at[y, z] if ref is gk_ref else ref.at[y, z, low]
        early.append(
            go(remote(block, block, r_send.at[index, 4], r_recv.at[index, 4], up if way == 0 else down))
        )
    hop_single(0)
    tables(page_ref, length_ref, group_ref, freq_ref, cos_ref, sin_ref, bias_ref, offset_ref)
    hop(0)
    for copy in swaps[0]:
        copy.wait_recv()
    across = [
        go(remote(qa_ref.at[x], qa_ref.at[x], x_send.at[i], x_recv.at[i], to)) for i, to in enumerate((east, west))
    ]
    prepare(x)
    hop(1)
    relays = []
    for i, to in enumerate((east, west)):
        across[i].wait_recv()
        half = qa_ref.at[(x + NX - 1) % NX if i == 0 else (x + 1) % NX, pl.ds(i * (TOK // 2), TOK // 2), :]
        relays.append(go(remote(half, half, x_send.at[2 + i], x_recv.at[2 + i], to)))
    for copy in swaps[1] + swaps[2]:
        copy.wait_recv()
    newv_ref[...] = v2_ref[1]
    prepare((x + 1) % NX)
    prepare((x + 3) % NX)
    receive_values(0, [y])
    receive_values(1, [ahead(1), ahead(7)])
    for copy in relays:
        copy.wait_recv()
    prepare((x + 2) % NX)
    absorb([y], True)
    hop(2)
    absorb([ahead(1), ahead(7)])
    receive_values(2, [ahead(2), ahead(6)])
    absorb([ahead(2)])
    hop(3)
    shifts = [
        go(remote(ref.at[1], ref.at[0], s_send.at[i], s_recv.at[i], after)) for i, ref in enumerate((k2_ref, v2_ref))
    ]
    absorb([ahead(6)])
    receive_values(3, [ahead(3), ahead(5)])
    absorb([ahead(3), ahead(5)])
    hop(4)
    receive_values(4, [ahead(4)])

    def hand_over(j):
        b = (x + NX - 1 - j) % NX
        to = (b * COL + col, t)
        return [
            remote(stat_ref.at[b], rs_ref.at[j], t_send.at[j], t_recv.at[j], to),
            remote(o_ref.at[b], ro_ref.at[j], o_send.at[j], o_recv.at[j], to),
        ]

    def close(j, carry):
        b = (x + NX - 1 - j) % NX
        for h in range(HEADS):
            top, total, summed = update(b, h, [ahead(4)], False)
            o_ref[b, h * HD : (h + 1) * HD, :] = (summed / total).astype(jnp.bfloat16)
            stat_ref[b, h : h + 1, :] = top
            stat_ref[b, HEADS + h : HEADS + h + 1, :] = total
            if h == 0:

                @pl.when(j > 0)
                def _():
                    for copy in hand_over(j - 1):
                        copy.start()

        return carry

    lax.fori_loop(0, NX, close, 0)

    for copy in shifts:
        copy.wait_recv()
    for b in range(2):
        turned = turn(k2_ref[b].astype(jnp.float32).T, cos_ref[b], sin_ref[b])
        ks_ref[b * TOK : (b + 1) * TOK, :] = turned.T.astype(jnp.bfloat16)
        vs_ref[:, b * TOK : (b + 1) * TOK] = v2_ref[b].astype(jnp.float32).T.astype(jnp.bfloat16)
    newk_ref[...] = ks_ref[TOK:, :]
    columns = qt_ref[x]
    token = lax.broadcasted_iota(jnp.int32, (2 * TOK, TOK), 1) + TOK
    key = lax.broadcasted_iota(jnp.int32, (2 * TOK, TOK), 0)
    allowed = (key <= token) & (key >= token - offset_ref[...])
    suffix = []
    for h in range(HEADS):
        lane = (h // 2) * 128
        scores = jnp.dot(ks_ref[:, lane : lane + 256], widen(columns, h), preferred_element_type=jnp.float32)
        scores = [jnp.where(allowed, scores, NEG)]
        top = peak(scores)
        total, summed = weigh(scores, top, [vs_ref[h * HD : (h + 1) * HD, :]])
        suffix.append((top, total, summed / total))

    copies = [copy for j in range(NX - 1) for copy in hand_over(j)]
    for copy in copies:
        copy.wait_recv()
    heads = []
    for h in range(HEADS):
        part = slice(h * HD, (h + 1) * HD)
        one, two = slice(h, h + 1), slice(HEADS + h, HEADS + h + 1)
        tops = [suffix[h][0], stat_ref[x, one, :]] + [rs_ref[j, one, :] for j in range(NX - 1)]
        totals = [suffix[h][1], stat_ref[x, two, :]] + [rs_ref[j, two, :] for j in range(NX - 1)]
        outs = [suffix[h][2], o_ref[x, part, :]] + [ro_ref[j, part, :] for j in range(NX - 1)]
        top = tops[0]
        for other in tops[1:]:
            top = jnp.maximum(top, other)
        scales = [jnp.exp2((a - top) * EXP_SCALE) * b for a, b in zip(tops, totals)]
        total = scales[0] + scales[1] + scales[2] + scales[3] + scales[4]
        acc = outs[0] * (scales[0] / total)
        for out, scale in zip(outs[1:], scales[1:]):
            acc += out.astype(jnp.float32) * (scale / total)
        heads.append(acc)
    c_ref[...] = jnp.concatenate(heads, axis=0).T.astype(jnp.bfloat16)

    def out_rows(index):
        return c_ref.at[pl.ds(pl.multiple_of(index * PART, PART), PART), :]

    place = out_ref.at[:, pl.ds(pl.multiple_of(t * CH, 128), CH)]
    back = [remote(out_rows(tps[j][1]), place, b_send.at[j], b_recv.at[j], tps[j]) for j in range(NT - 1)]
    for copy in back:
        copy.start()
    mine = pltpu.make_async_copy(out_rows(t), place, loc.at[5])
    mine.start()
    mine.wait()
    for copy in back:
        copy.wait_recv()
    for copy in pending + copies + back:
        copy.wait_send()


def attend(q, k, v, pk, pv, pages, lengths, groups):
    f32, bf = jnp.float32, jnp.bfloat16
    inverse_freq = (10000.0 ** (-(np.arange(HALF) * 2.0 / ROT))).astype(np.float32)
    freq = jnp.asarray(np.concatenate([inverse_freq, inverse_freq])[:, None])
    dma = pltpu.SemaphoreType.DMA
    return pl.pallas_call(
        attend_kernel,
        out_shape=(
            jax.ShapeDtypeStruct((PART, NT * CH), bf),
            jax.ShapeDtypeStruct((TOK, CH), bf),
            jax.ShapeDtypeStruct((TOK, CH), bf),
        ),
        in_specs=[pl.BlockSpec(memory_space=VMEM)] * 9,
        out_specs=[pl.BlockSpec(memory_space=VMEM)] * 3,
        scratch_shapes=[
            VMEM((2 + NX, ROT, TOK), f32),
            VMEM((2 + NX, ROT, TOK), f32),
            VMEM((NX, NY, NZ, TOK), f32),
            VMEM((1, TOK), jnp.int32),
            VMEM((NX, TOK, CH), bf),
            VMEM((2, TOK, CH), bf),
            VMEM((2, TOK, CH), bf),
            VMEM((NY, NZ, PAGE, CH), bf),
            VMEM((NY, NZ, PAGE, CH), bf),
            VMEM((NX, CH, TOK), bf),
            VMEM((NY, CH, NZ * PAGE), bf),
            VMEM((CH, 2 * TOK), bf),
            VMEM((2 * TOK, CH), bf),
            VMEM((NX, CH, TOK), f32),
            VMEM((NX, 2 * HEADS, TOK), f32),
            VMEM((NX, CH, TOK), bf),
            VMEM((NX, 2 * HEADS, TOK), f32),
            VMEM((NX - 1, CH, TOK), bf),
            VMEM((NX - 1, 2 * HEADS, TOK), f32),
            VMEM((TOK, CH), bf),
            dma((3, NT - 1)), dma((3, NT - 1)),
            dma((2,)), dma((2,)),
            dma((4, 5)), dma((4, 5)),
            dma((4, 5)), dma((4, 5)),
            dma((4,)), dma((4,)),
            dma((2,)), dma((2,)),
            dma((NX - 1,)), dma((NX - 1,)),
            dma((NX - 1,)), dma((NX - 1,)),
            dma((NT - 1,)), dma((NT - 1,)),
            dma((6,)),
        ],
        compiler_params=pltpu.CompilerParams(collective_id=0, has_side_effects=True),
        name="attend",
    )(q, k, v, pk, pv, pages, lengths, groups, freq)


def local(queries, keys, values, pool_keys, pool_values, page_table, lengths, group_of):
    return attend(
        queries, keys, values, pool_keys, pool_values, page_table[None, :], lengths[None, :], group_of[None, :]
    )


def solution(mesh):
    return jax.shard_map(
        local,
        mesh=mesh,
        in_specs=(
            P(("seq", "tp"), None),
            P(("seq", "tp"), None),
            P(("seq", "tp"), None),
            P("seq", None, "tp"),
            P("seq", None, "tp"),
            P(),
            P(),
            P(),
        ),
        out_specs=(P(("seq", "tp"), None), P("seq", "tp"), P("seq", "tp")),
        check_vma=False,
    )
```

```python
import jax
import jax.numpy as jnp
import numpy as np
from jax import lax
from jax.experimental import pallas as pl
from jax.experimental.pallas import tpu as pltpu
from jax.sharding import PartitionSpec as P

MESH = pl.DeviceIdType.MESH
HD = 96
ROT = 24
HALF = ROT // 2
HEADS = 4
CH = HEADS * HD
TOK = 256
PART = 32
NT = 8
NX, NY, NZ = 4, 8, 2
COL = NY * NZ
PAGE = 128
KEYS = COL * PAGE
SEQ = NX * NY * NZ
NEG = -1e30
EXP_SCALE = HD**-0.5 * 1.4426950408889634
VMEM = pltpu.VMEM


def where_am_i():
    s = lax.axis_index("seq")
    t = lax.axis_index("tp")
    x = s // COL
    y = (s // NZ) % NY
    z = s % NZ
    return s, t, x, y, z


def greet(peers):
    barrier = pltpu.get_barrier_semaphore()
    for peer in peers:
        pl.semaphore_signal(barrier, inc=1, device_id=peer, device_id_type=MESH)
    pl.semaphore_wait(barrier, len(peers))


def remote(src, dst, send, recv, peer):
    return pltpu.make_async_remote_copy(
        src_ref=src, dst_ref=dst, send_sem=send, recv_sem=recv, device_id=peer, device_id_type=MESH
    )


def turn(matrix, cosine, sine):
    parts = []
    for h in range(HEADS):
        lead = matrix[h * HD : h * HD + ROT]
        other = jnp.concatenate([lead[HALF:], lead[:HALF]], axis=0)
        parts += [lead * cosine + other * sine, matrix[h * HD + ROT : (h + 1) * HD]]
    return jnp.concatenate(parts, axis=0)


def widen(columns, h):
    start = h * HD - (h // 2) * 128
    pieces = []
    if start:
        pieces.append(jnp.zeros((start, TOK), jnp.bfloat16))
    pieces.append(columns[h * HD : (h + 1) * HD])
    if start + HD < 256:
        pieces.append(jnp.zeros((256 - start - HD, TOK), jnp.bfloat16))
    return jnp.concatenate(pieces, axis=0)


def tables(page_ref, length_ref, group_ref, freq_ref, cos_ref, sin_ref, bias_ref, offset_ref):
    s, t, x, y, z = where_am_i()
    f32 = jnp.float32
    count = length_ref.shape[1]
    slots = page_ref.shape[1]
    lane = lax.broadcasted_iota(jnp.int32, (count, count), 1)
    line = lax.broadcasted_iota(jnp.int32, (count, count), 0)
    lengths = jnp.broadcast_to(length_ref[...].astype(f32), (count, count))
    groups = jnp.broadcast_to(group_ref[...].astype(f32), (count, count))
    starts = jnp.sum(jnp.where(lane < line, lengths, 0.0), axis=1, keepdims=True)
    ends = jnp.sum(jnp.where(lane <= line, lengths, 0.0), axis=1, keepdims=True)
    group_of = jnp.sum(jnp.where(lane == line, groups, 0.0), axis=1, keepdims=True)
    slot = lax.broadcasted_iota(jnp.int32, (COL, slots), 0) + x * COL
    place = lax.broadcasted_iota(jnp.int32, (COL, slots), 1)
    page = jnp.broadcast_to(page_ref[...], (COL, slots))
    late = jnp.sum(jnp.where((page == slot) & (place >= slots // 2), 1.0, 0.0), axis=1, keepdims=True)
    sign = jnp.where(lax.broadcasted_iota(jnp.int32, (ROT, TOK), 0) < HALF, -1.0, 1.0)
    for i in range(2 + NX):
        block = s - 1 + i if i < 2 else (i - 2) * COL + s % COL
        rows = (block * TOK + lax.broadcasted_iota(jnp.int32, (1, TOK), 1)).astype(f32)
        begun = starts <= rows
        first = jnp.max(jnp.where(begun, starts, 0.0), axis=0, keepdims=True)
        group = jnp.sum(jnp.where(begun & (rows < ends), group_of, 0.0), axis=0, keepdims=True)
        offset = rows - first
        angles = (COL * NX * PAGE // 2 + offset) * freq_ref[...]
        cos_ref[i] = jnp.cos(angles)
        sin_ref[i] = jnp.sin(angles) * sign
        if i == 1:
            offset_ref[...] = offset.astype(jnp.int32)
        if i >= 2:
            bias = jnp.where(group == late, 0.0, NEG)
            for at in range(NY):
                bias_ref[i - 2, at] = bias[at * NZ : (at + 1) * NZ]


def attend_kernel(
    q_ref, k_ref, v_ref, pk_ref, pv_ref, page_ref, length_ref, group_ref, freq_ref,
    out_ref, newk_ref, newv_ref,
    cos_ref, sin_ref, bias_ref, offset_ref,
    qa_ref, k2_ref, v2_ref, gk_ref, gv_ref,
    qt_ref, vt_ref, vs_ref, ks_ref, acc_ref, run_ref, o_ref, stat_ref, ro_ref, rs_ref, rl_ref, c_ref,
    a_send, a_recv, z_send, z_recv, r_send, r_recv, y_send, y_recv, x_send, x_recv, s_send, s_recv,
    o_send, o_recv, f_send, f_recv, t_send, t_recv, b_send, b_recv, loc,
):
    s, t, x, y, z = where_am_i()
    col = s % COL
    partner = (s + 1 - 2 * z, t)
    up = (x * COL + ((y + 1) % NY) * NZ + z, t)
    down = (x * COL + ((y + NY - 1) % NY) * NZ + z, t)
    east = (((x + 1) % NX) * COL + col, t)
    west = (((x + NX - 1) % NX) * COL + col, t)
    across_x = (((x + 2) % NX) * COL + col, t)
    after = ((s + 1) % SEQ, t)
    before = ((s + SEQ - 1) % SEQ, t)
    tps = [(s, (t + j) % NT) for j in range(1, NT)]
    greet([partner, up, down, east, west, across_x, after, before] + tps)

    pending = []

    def go(copy):
        copy.start()
        pending.append(copy)
        return copy

    low, high = pl.ds(0, PAGE // 2), pl.ds(PAGE // 2, PAGE // 2)
    zk = go(remote(pk_ref.at[0], gk_ref.at[y, z], z_send.at[0], z_recv.at[0], partner))
    zv = go(remote(pv_ref.at[0, low], gv_ref.at[y, z, low], z_send.at[1], z_recv.at[1], partner))

    def rows(ref, kind):
        return ref.at[x if kind == 0 else 1, pl.ds(pl.multiple_of(t * PART, PART), PART), :]

    def lanes(ref, index):
        return ref.at[:, pl.ds(pl.multiple_of(index * CH, 128), CH)]

    kinds = [(q_ref, qa_ref), (k_ref, k2_ref), (v_ref, v2_ref)]
    own = [
        pltpu.make_async_copy(pk_ref.at[0], gk_ref.at[y, z], loc.at[0]),
        pltpu.make_async_copy(pv_ref.at[0], gv_ref.at[y, z], loc.at[1]),
    ] + [
        pltpu.make_async_copy(lanes(src, t), rows(dst, kind), loc.at[2 + kind])
        for kind, (src, dst) in enumerate(kinds)
    ]
    for copy in own:
        copy.start()

    def swap(kind):
        src, dst = kinds[kind]
        return [
            go(remote(lanes(src, tps[j][1]), rows(dst, kind), a_send.at[kind, j], a_recv.at[kind, j], tps[j]))
            for j in range(NT - 1)
        ]

    query_swap = swap(0)
    for copy in own:
        copy.wait()

    flows = [(gk_ref, 0, 4), (gv_ref, 0, 3), (gk_ref, 1, 3), (gv_ref, 1, 4)]
    last = [None] * len(flows)
    single = [None, None]
    handed = {}

    def index_of(way, step):
        return (y + NY - step) % NY if way == 0 else (y + step) % NY

    def hop_single(step):
        for way, hops in ((0, 4), (1, 3)):
            block = gv_ref.at[index_of(way, step), z, high]
            if single[way] is not None:
                single[way].wait_recv()
                single[way] = None
            if step < hops:
                single[way] = go(
                    remote(block, block, y_send.at[way, step], y_recv.at[way, step], up if way == 0 else down)
                )
            if step <= hops and (way == 0 or step > 0):
                handed.setdefault(step, []).append(
                    go(remote(block, block, y_send.at[2 + way, step], y_recv.at[2 + way, step], partner))
                )

    def hop(step):
        if step > 0:
            hop_single(step)
        else:
            zk.wait_recv()
            zv.wait_recv()
        for index, (ref, way, hops) in enumerate(flows):
            if last[index] is not None:
                last[index].wait_recv()
                last[index] = None
            if step == 1:
                early[index].wait_recv()
            if step < hops:
                at = index_of(way, step)
                which = 1 - z if step == 0 else slice(None)
                block = ref.at[at, which] if ref is gk_ref else ref.at[at, which, low]
                last[index] = go(
                    remote(block, block, r_send.at[index, step], r_recv.at[index, step], up if way == 0 else down)
                )

    def prepare(b):
        turned = turn(qa_ref[b].astype(jnp.float32).T, cos_ref[2 + b], sin_ref[2 + b])
        qt_ref[b] = turned.astype(jnp.bfloat16)

    def receive_values(step, places):
        for copy in handed.pop(step, []):
            copy.wait_recv()
        for at in places:
            vt_ref[at] = gv_ref[at].reshape(NZ * PAGE, CH).astype(jnp.float32).T.astype(jnp.bfloat16)

    def score(b, h, at):
        lane = (h // 2) * 128
        keys = gk_ref[at, :, :, lane : lane + 256].reshape(NZ * PAGE, 256)
        scores = jnp.dot(keys, widen(qt_ref[b], h), preferred_element_type=jnp.float32)
        return (scores.reshape(NZ, PAGE, TOK) + bias_ref[b, at][:, None, :]).reshape(NZ * PAGE, TOK)

    def weigh(scores, top, values):
        total, summed = None, None
        for block, value in zip(scores, values):
            weights = jnp.exp2((block - top) * EXP_SCALE)
            part = jnp.sum(weights, axis=0, keepdims=True)
            out = jnp.dot(value, weights.astype(jnp.bfloat16), preferred_element_type=jnp.float32)
            total = part if total is None else total + part
            summed = out if summed is None else summed + out
        return total, summed

    def peak(scores):
        top = jnp.max(scores[0], axis=0, keepdims=True)
        for block in scores[1:]:
            top = jnp.maximum(top, jnp.max(block, axis=0, keepdims=True))
        return top

    def update(b, h, places, first):
        part = slice(h * HD, (h + 1) * HD)
        scores = [score(b, h, at) for at in places]
        top = peak(scores)
        if not first:
            old = run_ref[b, h : h + 1, :]
            top = jnp.maximum(old, top)
        total, summed = weigh(scores, top, [vt_ref[at, part, :] for at in places])
        if not first:
            factor = jnp.exp2((old - top) * EXP_SCALE)
            total += run_ref[b, HEADS + h : HEADS + h + 1, :] * factor
            summed += acc_ref[b, part, :] * factor
        return top, total, summed

    def absorb(places, first=False):
        def one(b, carry):
            for h in range(HEADS):
                top, total, summed = update(b, h, places, first)
                run_ref[b, h : h + 1, :] = top
                run_ref[b, HEADS + h : HEADS + h + 1, :] = total
                acc_ref[b, h * HD : (h + 1) * HD, :] = summed
            return carry

        lax.fori_loop(0, NX, one, 0)

    def ahead(n):
        return (y + n) % NY

    early = []
    for index, (ref, way, hops) in enumerate(flows):
        block = ref.at[y, z] if ref is gk_ref else ref.at[y, z, low]
        early.append(
            go(remote(block, block, r_send.at[index, 4], r_recv.at[index, 4], up if way == 0 else down))
        )
    hop_single(0)
    tables(page_ref, length_ref, group_ref, freq_ref, cos_ref, sin_ref, bias_ref, offset_ref)
    hop(0)
    for copy in query_swap:
        copy.wait_recv()
    across = [
        go(remote(qa_ref.at[x], qa_ref.at[x], x_send.at[i], x_recv.at[i], to)) for i, to in enumerate((east, west))
    ]
    other_swaps = swap(1) + swap(2)
    hop(1)
    relays = []
    for i, to in enumerate((east, west)):
        across[i].wait_recv()
        half = qa_ref.at[(x + NX - 1) % NX if i == 0 else (x + 1) % NX, pl.ds(i * (TOK // 2), TOK // 2), :]
        relays.append(go(remote(half, half, x_send.at[2 + i], x_recv.at[2 + i], to)))
    prepare(x)
    prepare((x + 1) % NX)
    prepare((x + 3) % NX)
    receive_values(0, [y])
    for copy in relays:
        copy.wait_recv()
    prepare((x + 2) % NX)
    hop(2)
    absorb([y], True)
    receive_values(1, [ahead(1), ahead(7)])
    absorb([ahead(1), ahead(7)])
    hop(3)
    for copy in other_swaps:
        copy.wait_recv()
    shifts = [
        go(remote(ref.at[1], ref.at[0], s_send.at[i], s_recv.at[i], after)) for i, ref in enumerate((k2_ref, v2_ref))
    ]
    newv_ref[...] = v2_ref[1]
    receive_values(2, [ahead(2), ahead(6)])
    absorb([ahead(2), ahead(6)])
    hop(4)
    receive_values(3, [ahead(3), ahead(5)])
    absorb([ahead(3), ahead(5)])
    receive_values(4, [ahead(4)])

    def hand_stat(slot):
        b = (x + NX - 1 - slot) % NX
        return remote(stat_ref.at[b], rs_ref.at[slot], t_send.at[slot], t_recv.at[slot], (b * COL + col, t))

    def hand_near(slot):
        b = (x + NX - 1 - slot) % NX
        return remote(o_ref.at[b], ro_ref.at[slot], o_send.at[slot], o_recv.at[slot], (b * COL + col, t))

    def hand_far(i):
        half = o_ref.at[(x + 2) % NX, pl.ds(i * (CH // 2), CH // 2), :]
        return remote(half, rl_ref.at[i], f_send.at[i], f_recv.at[i], (east, west)[i])

    def pass_on(i):
        place = ro_ref.at[1, pl.ds(i * (CH // 2), CH // 2), :]
        return remote(rl_ref.at[i], place, f_send.at[2 + i], f_recv.at[2 + i], (east, west)[i])

    def close(j, carry):
        b = (x + 2 + j) % NX
        for h in range(HEADS):
            top, total, summed = update(b, h, [ahead(4)], False)
            o_ref[b, h * HD : (h + 1) * HD, :] = (summed / total).astype(jnp.bfloat16)
            stat_ref[b, h : h + 1, :] = top
            stat_ref[b, HEADS + h : HEADS + h + 1, :] = total
            if h == 0:

                @pl.when(j == 1)
                def _():
                    for copy in (hand_far(0), hand_far(1), hand_stat(1)):
                        copy.start()

                @pl.when(j == 2)
                def _():
                    for copy in (hand_near(0), hand_stat(0)):
                        copy.start()

        return carry

    lax.fori_loop(0, NX, close, 0)

    for copy in shifts:
        copy.wait_recv()
    for b in range(2):
        turned = turn(k2_ref[b].astype(jnp.float32).T, cos_ref[b], sin_ref[b])
        ks_ref[b * TOK : (b + 1) * TOK, :] = turned.T.astype(jnp.bfloat16)
        vs_ref[:, b * TOK : (b + 1) * TOK] = v2_ref[b].astype(jnp.float32).T.astype(jnp.bfloat16)
        if b == 0:
            for copy in (hand_near(2), hand_stat(2)):
                copy.start()
    newk_ref[...] = ks_ref[TOK:, :]
    for i in range(2):
        hand_far(i).wait_recv()
        pass_on(i).start()
    columns = qt_ref[x]
    token = lax.broadcasted_iota(jnp.int32, (2 * TOK, TOK), 1) + TOK
    key = lax.broadcasted_iota(jnp.int32, (2 * TOK, TOK), 0)
    allowed = (key <= token) & (key >= token - offset_ref[...])
    suffix = []
    for h in range(HEADS):
        lane = (h // 2) * 128
        scores = jnp.dot(ks_ref[:, lane : lane + 256], widen(columns, h), preferred_element_type=jnp.float32)
        scores = [jnp.where(allowed, scores, NEG)]
        top = peak(scores)
        total, summed = weigh(scores, top, [vs_ref[h * HD : (h + 1) * HD, :]])
        suffix.append((top, total, summed / total))

    far = [hand_far(0), hand_far(1)]
    copies = [hand_near(0), hand_near(2), pass_on(0), pass_on(1)] + [hand_stat(slot) for slot in range(NX - 1)]
    for copy in copies:
        copy.wait_recv()
    heads = []
    for h in range(HEADS):
        part = slice(h * HD, (h + 1) * HD)
        one, two = slice(h, h + 1), slice(HEADS + h, HEADS + h + 1)
        tops = [suffix[h][0], stat_ref[x, one, :]] + [rs_ref[j, one, :] for j in range(NX - 1)]
        totals = [suffix[h][1], stat_ref[x, two, :]] + [rs_ref[j, two, :] for j in range(NX - 1)]
        outs = [suffix[h][2], o_ref[x, part, :]] + [ro_ref[j, part, :] for j in range(NX - 1)]
        top = tops[0]
        for other in tops[1:]:
            top = jnp.maximum(top, other)
        scales = [jnp.exp2((a - top) * EXP_SCALE) * b for a, b in zip(tops, totals)]
        total = scales[0] + scales[1] + scales[2] + scales[3] + scales[4]
        acc = outs[0] * (scales[0] / total)
        for out, scale in zip(outs[1:], scales[1:]):
            acc += out.astype(jnp.float32) * (scale / total)
        heads.append(acc)
    c_ref[...] = jnp.concatenate(heads, axis=0).T.astype(jnp.bfloat16)

    def out_rows(index):
        return c_ref.at[pl.ds(pl.multiple_of(index * PART, PART), PART), :]

    place = out_ref.at[:, pl.ds(pl.multiple_of(t * CH, 128), CH)]
    back = [remote(out_rows(tps[j][1]), place, b_send.at[j], b_recv.at[j], tps[j]) for j in range(NT - 1)]
    for copy in back:
        copy.start()
    mine = pltpu.make_async_copy(out_rows(t), place, loc.at[5])
    mine.start()
    mine.wait()
    for copy in back:
        copy.wait_recv()
    for copy in pending + far + copies + back:
        copy.wait_send()


def attend(q, k, v, pk, pv, pages, lengths, groups):
    f32, bf = jnp.float32, jnp.bfloat16
    inverse_freq = (10000.0 ** (-(np.arange(HALF) * 2.0 / ROT))).astype(np.float32)
    freq = jnp.asarray(np.concatenate([inverse_freq, inverse_freq])[:, None])
    dma = pltpu.SemaphoreType.DMA
    return pl.pallas_call(
        attend_kernel,
        out_shape=(
            jax.ShapeDtypeStruct((PART, NT * CH), bf),
            jax.ShapeDtypeStruct((TOK, CH), bf),
            jax.ShapeDtypeStruct((TOK, CH), bf),
        ),
        in_specs=[pl.BlockSpec(memory_space=VMEM)] * 9,
        out_specs=[pl.BlockSpec(memory_space=VMEM)] * 3,
        scratch_shapes=[
            VMEM((2 + NX, ROT, TOK), f32),
            VMEM((2 + NX, ROT, TOK), f32),
            VMEM((NX, NY, NZ, TOK), f32),
            VMEM((1, TOK), jnp.int32),
            VMEM((NX, TOK, CH), bf),
            VMEM((2, TOK, CH), bf),
            VMEM((2, TOK, CH), bf),
            VMEM((NY, NZ, PAGE, CH), bf),
            VMEM((NY, NZ, PAGE, CH), bf),
            VMEM((NX, CH, TOK), bf),
            VMEM((NY, CH, NZ * PAGE), bf),
            VMEM((CH, 2 * TOK), bf),
            VMEM((2 * TOK, CH), bf),
            VMEM((NX, CH, TOK), f32),
            VMEM((NX, 2 * HEADS, TOK), f32),
            VMEM((NX, CH, TOK), bf),
            VMEM((NX, 2 * HEADS, TOK), f32),
            VMEM((NX - 1, CH, TOK), bf),
            VMEM((NX - 1, 2 * HEADS, TOK), f32),
            VMEM((2, CH // 2, TOK), bf),
            VMEM((TOK, CH), bf),
            dma((3, NT - 1)), dma((3, NT - 1)),
            dma((2,)), dma((2,)),
            dma((4, 5)), dma((4, 5)),
            dma((4, 5)), dma((4, 5)),
            dma((4,)), dma((4,)),
            dma((2,)), dma((2,)),
            dma((NX - 1,)), dma((NX - 1,)),
            dma((4,)), dma((4,)),
            dma((NX - 1,)), dma((NX - 1,)),
            dma((NT - 1,)), dma((NT - 1,)),
            dma((6,)),
        ],
        compiler_params=pltpu.CompilerParams(collective_id=0, has_side_effects=True),
        name="attend",
    )(q, k, v, pk, pv, pages, lengths, groups, freq)


def local(queries, keys, values, pool_keys, pool_values, page_table, lengths, group_of):
    return attend(
        queries, keys, values, pool_keys, pool_values, page_table[None, :], lengths[None, :], group_of[None, :]
    )


def solution(mesh):
    return jax.shard_map(
        local,
        mesh=mesh,
        in_specs=(
            P(("seq", "tp"), None),
            P(("seq", "tp"), None),
            P(("seq", "tp"), None),
            P("seq", None, "tp"),
            P("seq", None, "tp"),
            P(),
            P(),
            P(),
        ),
        out_specs=(P(("seq", "tp"), None), P("seq", "tp"), P("seq", "tp")),
        check_vma=False,
    )
```

```python
import jax
import jax.numpy as jnp
import numpy as np
from jax import lax
from jax.experimental import pallas as pl
from jax.experimental.pallas import tpu as pltpu
from jax.sharding import PartitionSpec as P

MESH = pl.DeviceIdType.MESH
HD = 96
ROT = 24
HALF = ROT // 2
HEADS = 4
CH = HEADS * HD
TOK = 256
PART = 32
NT = 8
NX, NY, NZ = 4, 8, 2
COL = NY * NZ
PAGE = 128
KEYS = COL * PAGE
SEQ = NX * NY * NZ
NEG = -1e30
EXP_SCALE = HD**-0.5 * 1.4426950408889634
VMEM = pltpu.VMEM


def where_am_i():
    s = lax.axis_index("seq")
    t = lax.axis_index("tp")
    x = s // COL
    y = (s // NZ) % NY
    z = s % NZ
    return s, t, x, y, z


def greet(peers):
    barrier = pltpu.get_barrier_semaphore()
    for peer in peers:
        pl.semaphore_signal(barrier, inc=1, device_id=peer, device_id_type=MESH)
    pl.semaphore_wait(barrier, len(peers))


def remote(src, dst, send, recv, peer):
    return pltpu.make_async_remote_copy(
        src_ref=src, dst_ref=dst, send_sem=send, recv_sem=recv, device_id=peer, device_id_type=MESH
    )


def turn(matrix, cosine, sine):
    parts = []
    for h in range(HEADS):
        lead = matrix[h * HD : h * HD + ROT]
        other = jnp.concatenate([lead[HALF:], lead[:HALF]], axis=0)
        parts += [lead * cosine + other * sine, matrix[h * HD + ROT : (h + 1) * HD]]
    return jnp.concatenate(parts, axis=0)


def widen(columns, h):
    start = h * HD - (h // 2) * 128
    pieces = []
    if start:
        pieces.append(jnp.zeros((start, TOK), jnp.bfloat16))
    pieces.append(columns[h * HD : (h + 1) * HD])
    if start + HD < 256:
        pieces.append(jnp.zeros((256 - start - HD, TOK), jnp.bfloat16))
    return jnp.concatenate(pieces, axis=0)


def tables(page_ref, length_ref, group_ref, freq_ref, cos_ref, sin_ref, bias_ref, offset_ref):
    s, t, x, y, z = where_am_i()
    f32 = jnp.float32
    count = length_ref.shape[1]
    slots = page_ref.shape[1]
    lane = lax.broadcasted_iota(jnp.int32, (count, count), 1)
    line = lax.broadcasted_iota(jnp.int32, (count, count), 0)
    lengths = jnp.broadcast_to(length_ref[...].astype(f32), (count, count))
    groups = jnp.broadcast_to(group_ref[...].astype(f32), (count, count))
    starts = jnp.sum(jnp.where(lane < line, lengths, 0.0), axis=1, keepdims=True)
    ends = jnp.sum(jnp.where(lane <= line, lengths, 0.0), axis=1, keepdims=True)
    group_of = jnp.sum(jnp.where(lane == line, groups, 0.0), axis=1, keepdims=True)
    slot = lax.broadcasted_iota(jnp.int32, (COL, slots), 0) + x * COL
    place = lax.broadcasted_iota(jnp.int32, (COL, slots), 1)
    page = jnp.broadcast_to(page_ref[...], (COL, slots))
    late = jnp.sum(jnp.where((page == slot) & (place >= slots // 2), 1.0, 0.0), axis=1, keepdims=True)
    sign = jnp.where(lax.broadcasted_iota(jnp.int32, (ROT, TOK), 0) < HALF, -1.0, 1.0)
    for i in range(2 + NX):
        block = s - 1 + i if i < 2 else (i - 2) * COL + s % COL
        rows = (block * TOK + lax.broadcasted_iota(jnp.int32, (1, TOK), 1)).astype(f32)
        begun = starts <= rows
        first = jnp.max(jnp.where(begun, starts, 0.0), axis=0, keepdims=True)
        group = jnp.sum(jnp.where(begun & (rows < ends), group_of, 0.0), axis=0, keepdims=True)
        offset = rows - first
        angles = (COL * NX * PAGE // 2 + offset) * freq_ref[...]
        cos_ref[i] = jnp.cos(angles)
        sin_ref[i] = jnp.sin(angles) * sign
        if i == 1:
            offset_ref[...] = offset.astype(jnp.int32)
        if i >= 2:
            bias = jnp.where(group == late, 0.0, NEG)
            for at in range(NY):
                bias_ref[i - 2, at] = bias[at * NZ : (at + 1) * NZ]


def attend_kernel(
    q_ref, k_ref, v_ref, pk_ref, pv_ref, page_ref, length_ref, group_ref, freq_ref,
    out_ref, newk_ref, newv_ref,
    cos_ref, sin_ref, bias_ref, offset_ref,
    qa_ref, k2_ref, v2_ref, gk_ref, gv_ref,
    qt_ref, vt_ref, vs_ref, ks_ref, acc_ref, run_ref, o_ref, stat_ref, ro_ref, rs_ref, rl_ref, c_ref,
    a_send, a_recv, z_send, z_recv, r_send, r_recv, y_send, y_recv, x_send, x_recv, s_send, s_recv,
    o_send, o_recv, f_send, f_recv, t_send, t_recv, b_send, b_recv, loc,
):
    s, t, x, y, z = where_am_i()
    col = s % COL
    partner = (s + 1 - 2 * z, t)
    up = (x * COL + ((y + 1) % NY) * NZ + z, t)
    down = (x * COL + ((y + NY - 1) % NY) * NZ + z, t)
    east = (((x + 1) % NX) * COL + col, t)
    west = (((x + NX - 1) % NX) * COL + col, t)
    across_x = (((x + 2) % NX) * COL + col, t)
    after = ((s + 1) % SEQ, t)
    before = ((s + SEQ - 1) % SEQ, t)
    tps = [(s, (t + j) % NT) for j in range(1, NT)]
    greet([partner, up, down, east, west, across_x, after, before] + tps)

    pending = []

    def go(copy):
        copy.start()
        pending.append(copy)
        return copy

    low, high = pl.ds(0, PAGE // 2), pl.ds(PAGE // 2, PAGE // 2)
    zk = go(remote(pk_ref.at[0], gk_ref.at[y, z], z_send.at[0], z_recv.at[0], partner))
    zv = go(remote(pv_ref.at[0, low], gv_ref.at[y, z, low], z_send.at[1], z_recv.at[1], partner))

    def rows(ref, kind):
        return ref.at[x if kind == 0 else 1, pl.ds(pl.multiple_of(t * PART, PART), PART), :]

    def lanes(ref, index):
        return ref.at[:, pl.ds(pl.multiple_of(index * CH, 128), CH)]

    kinds = [(q_ref, qa_ref), (k_ref, k2_ref), (v_ref, v2_ref)]
    own = [
        pltpu.make_async_copy(pk_ref.at[0], gk_ref.at[y, z], loc.at[0]),
        pltpu.make_async_copy(pv_ref.at[0], gv_ref.at[y, z], loc.at[1]),
    ] + [
        pltpu.make_async_copy(lanes(src, t), rows(dst, kind), loc.at[2 + kind])
        for kind, (src, dst) in enumerate(kinds)
    ]
    for copy in own:
        copy.start()

    def swap(kind):
        src, dst = kinds[kind]
        return [
            go(remote(lanes(src, tps[j][1]), rows(dst, kind), a_send.at[kind, j], a_recv.at[kind, j], tps[j]))
            for j in range(NT - 1)
        ]

    query_swap = swap(0)
    for copy in own:
        copy.wait()

    flows = [(gk_ref, 0, 4), (gv_ref, 0, 3), (gk_ref, 1, 3), (gv_ref, 1, 4)]
    last = [None] * len(flows)
    single = [None, None]
    handed = {}

    def index_of(way, step):
        return (y + NY - step) % NY if way == 0 else (y + step) % NY

    def hop_single(step):
        for way, hops in ((0, 4), (1, 3)):
            block = gv_ref.at[index_of(way, step), z, high]
            if single[way] is not None:
                single[way].wait_recv()
                single[way] = None
            if step < hops:
                single[way] = go(
                    remote(block, block, y_send.at[way, step], y_recv.at[way, step], up if way == 0 else down)
                )
            if step <= hops and (way == 0 or step > 0):
                handed.setdefault(step, []).append(
                    go(remote(block, block, y_send.at[2 + way, step], y_recv.at[2 + way, step], partner))
                )

    def hop(step):
        if step > 0:
            hop_single(step)
        else:
            zk.wait_recv()
            zv.wait_recv()
        for index, (ref, way, hops) in enumerate(flows):
            if last[index] is not None:
                last[index].wait_recv()
                last[index] = None
            if step == 1:
                early[index].wait_recv()
            if step < hops:
                at = index_of(way, step)
                which = 1 - z if step == 0 else slice(None)
                block = ref.at[at, which] if ref is gk_ref else ref.at[at, which, low]
                last[index] = go(
                    remote(block, block, r_send.at[index, step], r_recv.at[index, step], up if way == 0 else down)
                )

    def prepare(b):
        turned = turn(qa_ref[b].astype(jnp.float32).T, cos_ref[2 + b], sin_ref[2 + b])
        qt_ref[b] = turned.astype(jnp.bfloat16)

    def receive_values(step, places):
        for copy in handed.pop(step, []):
            copy.wait_recv()
        for at in places:
            vt_ref[at] = gv_ref[at].reshape(NZ * PAGE, CH).astype(jnp.float32).T.astype(jnp.bfloat16)

    def score(b, h, at):
        lane = (h // 2) * 128
        keys = gk_ref[at, :, :, lane : lane + 256].reshape(NZ * PAGE, 256)
        scores = jnp.dot(keys, widen(qt_ref[b], h), preferred_element_type=jnp.float32)
        return (scores.reshape(NZ, PAGE, TOK) + bias_ref[b, at][:, None, :]).reshape(NZ * PAGE, TOK)

    def weigh(scores, top, values):
        total, summed = None, None
        for block, value in zip(scores, values):
            weights = jnp.exp2((block - top) * EXP_SCALE)
            part = jnp.sum(weights, axis=0, keepdims=True)
            out = jnp.dot(value, weights.astype(jnp.bfloat16), preferred_element_type=jnp.float32)
            total = part if total is None else total + part
            summed = out if summed is None else summed + out
        return total, summed

    def peak(scores):
        top = jnp.max(scores[0], axis=0, keepdims=True)
        for block in scores[1:]:
            top = jnp.maximum(top, jnp.max(block, axis=0, keepdims=True))
        return top

    def update(b, h, places, first):
        part = slice(h * HD, (h + 1) * HD)
        scores = [score(b, h, at) for at in places]
        top = peak(scores)
        if not first:
            old = run_ref[b, h : h + 1, :]
            top = jnp.maximum(old, top)
        total, summed = weigh(scores, top, [vt_ref[at, part, :] for at in places])
        if not first:
            factor = jnp.exp2((old - top) * EXP_SCALE)
            total += run_ref[b, HEADS + h : HEADS + h + 1, :] * factor
            summed += acc_ref[b, part, :] * factor
        return top, total, summed

    def absorb(places, first=False, start=0, stop=NX):
        def one(n, carry):
            b = (x + n) % NX
            for h in range(HEADS):
                top, total, summed = update(b, h, places, first)
                run_ref[b, h : h + 1, :] = top
                run_ref[b, HEADS + h : HEADS + h + 1, :] = total
                acc_ref[b, h * HD : (h + 1) * HD, :] = summed
            return carry

        lax.fori_loop(start, stop, one, 0)

    def ahead(n):
        return (y + n) % NY

    early = []
    for index, (ref, way, hops) in enumerate(flows):
        block = ref.at[y, z] if ref is gk_ref else ref.at[y, z, low]
        early.append(
            go(remote(block, block, r_send.at[index, 4], r_recv.at[index, 4], up if way == 0 else down))
        )
    hop_single(0)
    tables(page_ref, length_ref, group_ref, freq_ref, cos_ref, sin_ref, bias_ref, offset_ref)
    hop(0)
    for copy in query_swap:
        copy.wait_recv()
    across = [
        go(remote(qa_ref.at[x], qa_ref.at[x], x_send.at[i], x_recv.at[i], to)) for i, to in enumerate((east, west))
    ]
    other_swaps = swap(1) + swap(2)
    hop(1)
    prepare(x)
    receive_values(0, [y])
    relays = []
    for i, to in enumerate((east, west)):
        across[i].wait_recv()
        half = qa_ref.at[(x + NX - 1) % NX if i == 0 else (x + 1) % NX, pl.ds(i * (TOK // 2), TOK // 2), :]
        relays.append(go(remote(half, half, x_send.at[2 + i], x_recv.at[2 + i], to)))
    absorb([y], True, 0, 1)
    prepare((x + 1) % NX)
    absorb([y], True, 1, 2)
    prepare((x + 3) % NX)
    absorb([y], True, 3, 4)
    for copy in relays:
        copy.wait_recv()
    hop(2)
    prepare((x + 2) % NX)
    absorb([y], True, 2, 3)
    receive_values(1, [ahead(1), ahead(7)])
    absorb([ahead(1), ahead(7)])
    hop(3)
    for copy in other_swaps:
        copy.wait_recv()
    shifts = [
        go(remote(ref.at[1], ref.at[0], s_send.at[i], s_recv.at[i], after)) for i, ref in enumerate((k2_ref, v2_ref))
    ]
    newv_ref[...] = v2_ref[1]
    receive_values(2, [ahead(2), ahead(6)])
    absorb([ahead(2), ahead(6)])
    hop(4)
    receive_values(3, [ahead(3), ahead(5)])
    absorb([ahead(3), ahead(5)])
    receive_values(4, [ahead(4)])

    def hand_stat(slot):
        b = (x + NX - 1 - slot) % NX
        return remote(stat_ref.at[b], rs_ref.at[slot], t_send.at[slot], t_recv.at[slot], (b * COL + col, t))

    def hand_near(slot):
        b = (x + NX - 1 - slot) % NX
        return remote(o_ref.at[b], ro_ref.at[slot], o_send.at[slot], o_recv.at[slot], (b * COL + col, t))

    def hand_far(i):
        half = o_ref.at[(x + 2) % NX, pl.ds(i * (CH // 2), CH // 2), :]
        return remote(half, rl_ref.at[i], f_send.at[i], f_recv.at[i], (east, west)[i])

    def pass_on(i):
        place = ro_ref.at[1, pl.ds(i * (CH // 2), CH // 2), :]
        return remote(rl_ref.at[i], place, f_send.at[2 + i], f_recv.at[2 + i], (east, west)[i])

    def close(j, carry):
        b = (x + 2 + j) % NX
        for h in range(HEADS):
            top, total, summed = update(b, h, [ahead(4)], False)
            o_ref[b, h * HD : (h + 1) * HD, :] = (summed / total).astype(jnp.bfloat16)
            stat_ref[b, h : h + 1, :] = top
            stat_ref[b, HEADS + h : HEADS + h + 1, :] = total
            if h == 0:

                @pl.when(j == 1)
                def _():
                    for copy in (hand_far(0), hand_far(1), hand_stat(1)):
                        copy.start()

                @pl.when(j == 2)
                def _():
                    for copy in (hand_near(0), hand_stat(0)):
                        copy.start()

        return carry

    lax.fori_loop(0, NX, close, 0)

    for copy in shifts:
        copy.wait_recv()
    for b in range(2):
        turned = turn(k2_ref[b].astype(jnp.float32).T, cos_ref[b], sin_ref[b])
        ks_ref[b * TOK : (b + 1) * TOK, :] = turned.T.astype(jnp.bfloat16)
        vs_ref[:, b * TOK : (b + 1) * TOK] = v2_ref[b].astype(jnp.float32).T.astype(jnp.bfloat16)
        if b == 0:
            for copy in (hand_near(2), hand_stat(2)):
                copy.start()
    newk_ref[...] = ks_ref[TOK:, :]
    for i in range(2):
        hand_far(i).wait_recv()
        pass_on(i).start()
    columns = qt_ref[x]
    token = lax.broadcasted_iota(jnp.int32, (2 * TOK, TOK), 1) + TOK
    key = lax.broadcasted_iota(jnp.int32, (2 * TOK, TOK), 0)
    allowed = (key <= token) & (key >= token - offset_ref[...])
    suffix = []
    for h in range(HEADS):
        lane = (h // 2) * 128
        scores = jnp.dot(ks_ref[:, lane : lane + 256], widen(columns, h), preferred_element_type=jnp.float32)
        scores = [jnp.where(allowed, scores, NEG)]
        top = peak(scores)
        total, summed = weigh(scores, top, [vs_ref[h * HD : (h + 1) * HD, :]])
        suffix.append((top, total, summed / total))

    far = [hand_far(0), hand_far(1)]
    copies = [hand_near(0), hand_near(2), pass_on(0), pass_on(1)] + [hand_stat(slot) for slot in range(NX - 1)]
    for copy in copies:
        copy.wait_recv()
    heads = []
    for h in range(HEADS):
        part = slice(h * HD, (h + 1) * HD)
        one, two = slice(h, h + 1), slice(HEADS + h, HEADS + h + 1)
        tops = [suffix[h][0], stat_ref[x, one, :]] + [rs_ref[j, one, :] for j in range(NX - 1)]
        totals = [suffix[h][1], stat_ref[x, two, :]] + [rs_ref[j, two, :] for j in range(NX - 1)]
        outs = [suffix[h][2], o_ref[x, part, :]] + [ro_ref[j, part, :] for j in range(NX - 1)]
        top = tops[0]
        for other in tops[1:]:
            top = jnp.maximum(top, other)
        scales = [jnp.exp2((a - top) * EXP_SCALE) * b for a, b in zip(tops, totals)]
        total = scales[0] + scales[1] + scales[2] + scales[3] + scales[4]
        acc = outs[0] * (scales[0] / total)
        for out, scale in zip(outs[1:], scales[1:]):
            acc += out.astype(jnp.float32) * (scale / total)
        heads.append(acc)
    c_ref[...] = jnp.concatenate(heads, axis=0).T.astype(jnp.bfloat16)

    def out_rows(index):
        return c_ref.at[pl.ds(pl.multiple_of(index * PART, PART), PART), :]

    place = out_ref.at[:, pl.ds(pl.multiple_of(t * CH, 128), CH)]
    back = [remote(out_rows(tps[j][1]), place, b_send.at[j], b_recv.at[j], tps[j]) for j in range(NT - 1)]
    for copy in back:
        copy.start()
    mine = pltpu.make_async_copy(out_rows(t), place, loc.at[5])
    mine.start()
    mine.wait()
    for copy in back:
        copy.wait_recv()
    for copy in pending + far + copies + back:
        copy.wait_send()


def attend(q, k, v, pk, pv, pages, lengths, groups):
    f32, bf = jnp.float32, jnp.bfloat16
    inverse_freq = (10000.0 ** (-(np.arange(HALF) * 2.0 / ROT))).astype(np.float32)
    freq = jnp.asarray(np.concatenate([inverse_freq, inverse_freq])[:, None])
    dma = pltpu.SemaphoreType.DMA
    return pl.pallas_call(
        attend_kernel,
        out_shape=(
            jax.ShapeDtypeStruct((PART, NT * CH), bf),
            jax.ShapeDtypeStruct((TOK, CH), bf),
            jax.ShapeDtypeStruct((TOK, CH), bf),
        ),
        in_specs=[pl.BlockSpec(memory_space=VMEM)] * 9,
        out_specs=[pl.BlockSpec(memory_space=VMEM)] * 3,
        scratch_shapes=[
            VMEM((2 + NX, ROT, TOK), f32),
            VMEM((2 + NX, ROT, TOK), f32),
            VMEM((NX, NY, NZ, TOK), f32),
            VMEM((1, TOK), jnp.int32),
            VMEM((NX, TOK, CH), bf),
            VMEM((2, TOK, CH), bf),
            VMEM((2, TOK, CH), bf),
            VMEM((NY, NZ, PAGE, CH), bf),
            VMEM((NY, NZ, PAGE, CH), bf),
            VMEM((NX, CH, TOK), bf),
            VMEM((NY, CH, NZ * PAGE), bf),
            VMEM((CH, 2 * TOK), bf),
            VMEM((2 * TOK, CH), bf),
            VMEM((NX, CH, TOK), f32),
            VMEM((NX, 2 * HEADS, TOK), f32),
            VMEM((NX, CH, TOK), bf),
            VMEM((NX, 2 * HEADS, TOK), f32),
            VMEM((NX - 1, CH, TOK), bf),
            VMEM((NX - 1, 2 * HEADS, TOK), f32),
            VMEM((2, CH // 2, TOK), bf),
            VMEM((TOK, CH), bf),
            dma((3, NT - 1)), dma((3, NT - 1)),
            dma((2,)), dma((2,)),
            dma((4, 5)), dma((4, 5)),
            dma((4, 5)), dma((4, 5)),
            dma((4,)), dma((4,)),
            dma((2,)), dma((2,)),
            dma((NX - 1,)), dma((NX - 1,)),
            dma((4,)), dma((4,)),
            dma((NX - 1,)), dma((NX - 1,)),
            dma((NT - 1,)), dma((NT - 1,)),
            dma((6,)),
        ],
        compiler_params=pltpu.CompilerParams(collective_id=0, has_side_effects=True),
        name="attend",
    )(q, k, v, pk, pv, pages, lengths, groups, freq)


def local(queries, keys, values, pool_keys, pool_values, page_table, lengths, group_of):
    return attend(
        queries, keys, values, pool_keys, pool_values, page_table[None, :], lengths[None, :], group_of[None, :]
    )


def solution(mesh):
    return jax.shard_map(
        local,
        mesh=mesh,
        in_specs=(
            P(("seq", "tp"), None),
            P(("seq", "tp"), None),
            P(("seq", "tp"), None),
            P("seq", None, "tp"),
            P("seq", None, "tp"),
            P(),
            P(),
            P(),
        ),
        out_specs=(P(("seq", "tp"), None), P("seq", "tp"), P("seq", "tp")),
        check_vma=False,
    )
```
